32 devices in a mesh: shard: 4 (over z), tensor: 2 (over y), section: 4 (over x, core).
Axes of the slice: x: 2, y: 2, z: 4, core: 2. Of those that a mesh axis runs over, the one named last changes fastest.
Arguments:
- qkv_grad: bfloat16 [4, 4096, 6144], P('shard', 'section', 'tensor'), may hold values from -150 to 150
- master: float32 [4096, 6144], P(('section', 'shard', 'tensor')), may hold values from -3 to 3
- moment_one: float32 [4096, 6144], P(('section', 'shard', 'tensor')), may hold values from -3 to 3
- moment_two: float32 [4096, 6144], P(('section', 'shard', 'tensor')), may hold values from 0.05 to 2
- average: float32 [4096, 6144], P(('section', 'shard'), 'tensor'), may hold values from -3 to 3
- step: int32 [], replicated, may hold values from 1 to 20
Outputs:
- weights: bfloat16 [4096, 6144], P('section', 'tensor')
- new_master: float32 [4096, 6144], P(('section', 'shard', 'tensor'))
- new_one: float32 [4096, 6144], P(('section', 'shard', 'tensor'))
- new_two: float32 [4096, 6144], P(('section', 'shard', 'tensor'))
- new_average: float32 [4096, 6144], P(('section', 'shard'), 'tensor')
The draws below stay inside these ranges and needn't reach their ends.
All inputs are finite; a program needn't handle non-finite values.
Results may differ from the reference program's by a relative error of at most 0.0035.
Values may be sent and summed in bfloat16 or wider, within the bound.
A program may use at most 128 MiB of HBM per device.

```python
import math
import jax
import jax.numpy as jnp
from jax import lax

D = 4096
QKV = 6144
REPLICAS = 4


def draw_qkv_grad(key, part):
    base = jax.random.fold_in(key, 11)
    first, second, third = jax.random.split(base, 3)
    rows = jnp.arange(D).astype(jnp.float32)
    row_scale = jnp.power(jnp.float32(3.0), rows / D) * jnp.exp(jax.random.uniform(first, (D,), jnp.float32) * math.log(10.0))
    col_scale = jnp.exp(jax.random.uniform(second, (QKV,), jnp.float32) * math.log(10.0))
    noise = jnp.clip(jax.random.normal(third, (REPLICAS, D, QKV), jnp.float32), -5.0, 5.0)
    values = jnp.clip(noise * row_scale[None, :, None] * col_scale[None, None, :], -150.0, 150.0)
    return values.astype(jnp.bfloat16)


def levels(rng, extent, cuts, least, high):
    def one(dim, shards_of):
        draws = jax.random.uniform(jax.random.fold_in(jax.random.fold_in(rng, 6), dim), (shards_of,), jnp.float32, least / len(cuts), high / len(cuts))
        return jnp.repeat(jnp.exp(draws), extent[dim] // shards_of).reshape((-1,) + (1,) * (len(extent) - dim - 1))

    level = one(*cuts[0])
    for cut in cuts[1:]:
        level = level * one(*cut)
    return level


def centred(key, dims, width, reach, cuts=(), kind=jnp.bfloat16):
    entries = width * jax.random.normal(key, dims, jnp.float32)
    if cuts:
        entries = entries * levels(key, dims, cuts, -0.22, 0.18)
    return jnp.clip(entries, -reach, reach).astype(kind)


def setup_inputs(seed: int = 0) -> dict:
    key_list = jax.random.split(jax.random.key(seed), 7)
    return {
        "qkv_grad": draw_qkv_grad(jax.random.fold_in(key_list[6], 71), 0),
        "master": centred(key_list[1], (D, QKV), 0.5, 3.0, ((0, 32),), jnp.float32),
        "moment_one": centred(key_list[2], (D, QKV), 0.5, 3.0, ((0, 32),), jnp.float32),
        "moment_two": jnp.clip(jnp.exp(math.log(2.0) - 3.6888794 * jax.random.uniform(key_list[3], (D, QKV), jnp.float32) ** levels(key_list[3], (D, QKV), ((0, 32),), -0.2, 0.2)), 0.05, 2.0),
        "average": centred(key_list[4], (D, QKV), 0.5, 3.0, ((0, 16), (1, 2)), jnp.float32),
        "step": jax.random.randint(key_list[5], (), 1, 21).astype(jnp.int32),
    }


def reference(qkv_grad, master, moment_one, moment_two, average, step):
    grad = lax.optimization_barrier(jnp.sum(qkv_grad.astype(jnp.float32), axis=0))
    sumsq = jnp.sum(grad * grad)
    limit = jnp.float32(math.sqrt(D * QKV))
    clip = jnp.minimum(jnp.float32(1.0), limit / (jnp.sqrt(sumsq) + 1e-06))
    clipped = clip * grad
    new_one = 0.9 * moment_one + 0.1 * clipped
    new_two = 0.95 * moment_two + 0.05 * clipped * clipped
    count = step.astype(jnp.float32)
    first_fix = 1.0 - jnp.power(jnp.float32(0.9), count)
    second_fix = 1.0 - jnp.power(jnp.float32(0.95), count)
    update = new_one / first_fix / (jnp.sqrt(new_two / second_fix) + 1e-08)
    new_master = master * (1.0 - 0.1 * 0.1) - 0.1 * update
    weights = new_master.astype(jnp.bfloat16)
    new_average = 0.99 * average + 0.01 * new_master
    return (weights, new_master, new_one, new_two, new_average)
```

```python
import functools
import math

import jax
import jax.numpy as jnp
from jax import lax
from jax.experimental import pallas as pl
from jax.experimental.pallas import tpu as pltpu
from jax.sharding import PartitionSpec as P

MESH = pl.DeviceIdType.MESH
DEPTH = 4


def step_kernel(
    sizes, limit, step, x, master, one, two, average,
    w, out_master, out_one, out_two, out_average,
    held, inbox, gbox, half, square, zbox, pbox,
    x_sem, state_sem, hop_send, hop_recv, sum_send, sum_recv, z_send, z_recv, p_send, p_recv,
    y_send, y_recv, out_send, out_recv,
):
    shards, groups, sections = sizes
    s, t, c = lax.axis_index("shard"), lax.axis_index("tensor"), lax.axis_index("section")
    last = shards - 1
    near = shards // 2
    _, _, rows, cols = x.shape
    tile = inbox.shape[2]
    tiles = rows // tile
    share = groups * tiles
    count = near * share
    plane = groups * sections
    at_end = jnp.logical_or(s == 0, s == last)
    end = jnp.minimum(s, 1)

    def load(q, g):
        return pltpu.make_async_copy(x.at[q, g], held.at[q, g], x_sem.at[q, g])

    for n in range(near):
        for g in range(groups):
            @pl.when(s > 0)
            def _():
                load(near + n, g).start()

            @pl.when(s < last)
            def _():
                load(near - 1 - n, g).start()

    states = [
        pltpu.make_async_copy(src, dst, state_sem.at[n])
        for n, (src, dst) in enumerate(
            ((master, out_master), (one, out_one), (two, out_two), (average, out_average))
        )
    ]
    for copy in states:
        copy.start()

    barrier = pltpu.get_barrier_semaphore()

    def peer(off):
        at = lax.rem(t * sections + c + off, plane)
        return {"tensor": lax.div(at, sections), "section": lax.rem(at, sections)}

    @pl.loop(1, plane)
    def _(off):
        pl.semaphore_signal(barrier, inc=1, device_id=peer(off), device_id_type=MESH)

    @pl.loop(groups, shards * groups)
    def _(off):
        pl.semaphore_signal(
            barrier,
            inc=1,
            device_id={
                "shard": lax.rem(s + lax.div(off, groups), shards),
                "tensor": lax.rem(t + lax.rem(off, groups), groups),
            },
            device_id_type=MESH,
        )

    square[...] = jnp.zeros_like(square)
    zbox[...] = jnp.zeros_like(zbox)
    pl.semaphore_wait(barrier, plane - 1 + (shards - 1) * groups)

    def place(way, i):
        n, rest = lax.div(i, share), lax.rem(i, share)
        j, g = lax.div(rest, groups), lax.rem(rest, groups)
        return (near + n if way == 0 else near - 1 - n), g, j

    def part(j):
        return pl.ds(pl.multiple_of(j * tile, tile), tile)

    def hop(way, i, src):
        return pltpu.make_async_remote_copy(
            src_ref=src,
            dst_ref=inbox.at[way, i],
            send_sem=hop_send.at[way, i],
            recv_sem=hop_recv.at[way, i],
            device_id={"shard": jnp.minimum(s + 1, last) if way == 0 else jnp.maximum(s - 1, 0)},
            device_id_type=MESH,
        )

    def hand(way, i):
        q, g, j = place(way, i)
        return pltpu.make_async_remote_copy(
            src_ref=inbox.at[way, i],
            dst_ref=gbox.at[t, part(j)],
            send_sem=sum_send.at[i],
            recv_sem=sum_recv.at[t, j],
            device_id={"shard": q, "tensor": g},
            device_id_type=MESH,
        )

    def summed(g, j):
        return pltpu.make_async_remote_copy(
            src_ref=gbox.at[g, part(j)],
            dst_ref=gbox.at[g, part(j)],
            send_sem=sum_send.at[0],
            recv_sem=sum_recv.at[g, j],
            device_id={"tensor": g},
            device_id_type=MESH,
        )

    @pl.loop(0, count + last)
    def _(now):
        for way in (0, 1):
            lag = s if way == 0 else last - s
            i = now - lag
            q, g, j = place(way, i)

            @pl.when(jnp.logical_and(i >= 0, i < count))
            def _():
                @pl.when(jnp.logical_and(lag < last, i >= DEPTH))
                def _():
                    hop(way, i - DEPTH, inbox.at[way, i - DEPTH]).wait_send()

                @pl.when(lag == 0)
                def _():
                    hop(way, i, x.at[q, g, part(j)]).start()

                @pl.when(lag > 0)
                def _():
                    @pl.when(j == 0)
                    def _():
                        load(q, g).wait()

                    hop(way, i, inbox.at[way, i]).wait_recv()
                    acc = inbox[way, i].astype(jnp.float32) + held[q, g, part(j)].astype(jnp.float32)
                    short = acc.astype(jnp.bfloat16)

                    @pl.when(lag < last)
                    def _():
                        inbox[way, i] = short
                        hop(way, i, inbox.at[way, i]).start()

                    @pl.when(lag == last)
                    def _():
                        square[...] += jnp.sum((acc * acc).reshape(tile // 8, 8, cols), axis=0)
                        mine = jnp.logical_and(q == s, g == t)

                        @pl.when(mine)
                        def _():
                            gbox[t, part(j)] = short

                        @pl.when(jnp.logical_not(mine))
                        def _():
                            inbox[way, i] = short

                        @pl.when(jnp.logical_and(q == s, g != t))
                        def _():
                            hand(way, i).start()

    def spread(off):
        return pltpu.make_async_remote_copy(
            src_ref=zbox.at[end],
            dst_ref=zbox.at[end],
            send_sem=z_send.at[off],
            recv_sem=z_recv.at[end],
            device_id={"shard": lax.rem(s + off, shards)},
            device_id_type=MESH,
        )

    def level(off):
        return pltpu.make_async_remote_copy(
            src_ref=pbox.at[0],
            dst_ref=pbox.at[off],
            send_sem=p_send.at[off],
            recv_sem=p_recv.at[off],
            device_id=peer(off),
            device_id_type=MESH,
        )

    def came(slot):
        return pltpu.make_async_copy(zbox.at[slot], zbox.at[slot], z_recv.at[slot])

    @pl.when(at_end)
    def _():
        narrow = square[:, :128]
        for n in range(1, cols // 128):
            narrow = narrow + square[:, n * 128 : (n + 1) * 128]
        zbox[end] = narrow

        @pl.loop(1, shards)
        def _(off):
            spread(off).start()

    for way, where in ((0, last), (1, 0)):
        @pl.when(s == where)
        def _():
            @pl.loop(0, count - share)
            def _(i):
                hand(way, i).start()

    @pl.when(s > 0)
    def _():
        came(0).wait()

    @pl.when(s < last)
    def _():
        came(1).wait()

    pbox[0] = zbox[0] + zbox[1]

    @pl.loop(1, plane)
    def _(off):
        level(off).start()

    for way, here in ((0, s < last), (1, s > 0)):
        @pl.when(here)
        def _():
            @pl.loop(max(count - DEPTH, 0), count)
            def _(i):
                hop(way, i, inbox.at[way, i]).wait_send()

    for copy in states:
        copy.wait()
    times = jnp.full((8, 128), step[0].astype(jnp.float32))
    first_fix = jnp.max(1.0 / (1.0 - jnp.exp(times * math.log(0.9))))
    second_fix = jnp.max(1.0 / (1.0 - jnp.exp(times * math.log(0.95))))

    @pl.loop(1, plane)
    def _(off):
        level(off).wait_recv()

    whole = pbox[0]
    for n in range(1, plane):
        whole = whole + pbox[n]
    norm = jnp.sqrt(jnp.full((8, 128), jnp.sum(whole)))
    clip = jnp.max(jnp.minimum(1.0, limit / (norm + 1e-06)))

    def cross(k, j):
        return pltpu.make_async_remote_copy(
            src_ref=half.at[k, part(j)],
            dst_ref=w.at[s, t, part(j)],
            send_sem=y_send.at[k, j],
            recv_sem=y_recv.at[k, j],
            device_id={"tensor": lax.rem(t + k, groups)},
            device_id_type=MESH,
        )

    def crossed(k, j):
        g = lax.rem(t + k, groups)
        return pltpu.make_async_remote_copy(
            src_ref=w.at[s, g, part(j)],
            dst_ref=w.at[s, g, part(j)],
            send_sem=y_send.at[k, j],
            recv_sem=y_recv.at[groups - k, j],
            device_id={"tensor": g},
            device_id_type=MESH,
        )

    def forward(way, n):
        m = lax.rem(n, share)
        away = lax.div(n, share)
        p = s - away if way == 0 else s + away
        j, k = lax.div(m, groups), lax.rem(m, groups)
        block = w.at[p, lax.rem(t + k, groups), part(j)]
        return pltpu.make_async_remote_copy(
            src_ref=block,
            dst_ref=block,
            send_sem=out_send.at[way, p, m],
            recv_sem=out_recv.at[way, p, m],
            device_id={"shard": jnp.minimum(s + 1, last) if way == 0 else jnp.maximum(s - 1, 0)},
            device_id_type=MESH,
        )

    @pl.loop(0, shards * share + 1)
    def _(now):
        @pl.when(now < share)
        def _():
            j, k = lax.div(now, groups), lax.rem(now, groups)
            g = lax.rem(t + k, groups)
            there = pl.ds(pl.multiple_of(g * cols, 128), cols)

            @pl.when(jnp.logical_not(jnp.logical_and(at_end, k == 0)))
            def _():
                summed(g, j).wait_recv()

            clipped = clip * gbox[g, part(j)].astype(jnp.float32)
            new_one = 0.9 * out_one[part(j), there] + 0.1 * clipped
            new_two = 0.95 * out_two[part(j), there] + 0.05 * clipped * clipped
            update = new_one * first_fix / (jnp.sqrt(new_two * second_fix) + 1e-08)
            new_master = out_master[part(j), there] * (1.0 - 0.1 * 0.1) - 0.1 * update
            out_one[part(j), there] = new_one
            out_two[part(j), there] = new_two
            out_master[part(j), there] = new_master
            short = new_master.astype(jnp.bfloat16)

            @pl.when(k == 0)
            def _():
                w[s, t, part(j)] = short

            @pl.when(k > 0)
            def _():
                half[k, part(j)] = short
                cross(k, j).start()

        n = now - 1
        m = n - share

        @pl.when(jnp.logical_and(n >= 0, n < share))
        def _():
            j, k = lax.div(n, groups), lax.rem(n, groups)

            @pl.when(k > 0)
            def _():
                crossed(k, j).wait_recv()

        for way in (0, 1):
            reach = s if way == 0 else last - s
            inner = reach < 0 if shards == 1 else (s < last if way == 0 else s > 0)

            @pl.when(jnp.logical_and(n >= 0, n < (reach + 1) * share))
            def _():
                @pl.when(n >= share)
                def _():
                    forward(way, n).wait_recv()

                @pl.when(inner)
                def _():
                    forward(way, n).start()

                    @pl.when(n >= DEPTH)
                    def _():
                        forward(way, n - DEPTH).wait_send()

        @pl.when(jnp.logical_and(m >= 0, m < share))
        def _():
            j, g = lax.div(m, groups), lax.rem(m, groups)
            fresh = w[s, g, part(j)].astype(jnp.float32)
            out_average[g, part(j)] = 0.99 * out_average[g, part(j)] + 0.01 * fresh

    for way in (0, 1):
        reach = s if way == 0 else last - s

        @pl.when(s < last if way == 0 else s > 0)
        def _():
            @pl.loop(0, min(DEPTH, share))
            def _(n):
                forward(way, (reach + 1) * share - 1 - n).wait_send()

    for k in range(1, groups):
        @pl.loop(0, tiles)
        def _(j):
            cross(k, j).wait_send()

    for way, where in ((0, last), (1, 0)):
        @pl.when(s == where)
        def _():
            @pl.loop(0, count)
            def _(i):
                q, g, _ = place(way, i)

                @pl.when(jnp.logical_not(jnp.logical_and(q == s, g == t)))
                def _():
                    hand(way, i).wait_send()

    @pl.when(at_end)
    def _():
        @pl.loop(1, shards)
        def _(off):
            spread(off).wait_send()

    @pl.loop(1, plane)
    def _(off):
        level(off).wait_send()


def adam_step(sizes, limit, step, x, master, one, two, average):
    shards, groups, sections = sizes
    _, _, rows, cols = x.shape
    tile = min(rows, 16)
    tiles = rows // tile
    count = shards // 2 * groups * tiles
    plane = groups * sections
    dma = pltpu.SemaphoreType.DMA
    anywhere = pl.BlockSpec(memory_space=pl.ANY)
    near = pl.BlockSpec(memory_space=pltpu.VMEM)
    state = jax.ShapeDtypeStruct(master.shape, jnp.float32)
    return pl.pallas_call(
        functools.partial(step_kernel, sizes, limit),
        out_shape=[
            jax.ShapeDtypeStruct(x.shape, jnp.bfloat16),
            state,
            state,
            state,
            jax.ShapeDtypeStruct(average.shape, jnp.float32),
        ],
        in_specs=[pl.BlockSpec(memory_space=pltpu.SMEM)] + [anywhere] * 5,
        out_specs=[near] * 5,
        scratch_shapes=[
            pltpu.VMEM(x.shape, jnp.bfloat16),
            pltpu.VMEM((2, count, tile, cols), jnp.bfloat16),
            pltpu.VMEM((groups, rows, cols), jnp.bfloat16),
            pltpu.VMEM((groups, rows, cols), jnp.bfloat16),
            pltpu.VMEM((8, cols), jnp.float32),
            pltpu.VMEM((2, 8, 128), jnp.float32),
            pltpu.VMEM((plane, 8, 128), jnp.float32),
            dma((shards, groups)),
            dma((4,)),
            dma((2, count)),
            dma((2, count)),
            dma((count,)),
            dma((groups, tiles)),
            dma((shards,)),
            dma((2,)),
            dma((plane,)),
            dma((plane,)),
            dma((groups, tiles)),
            dma((groups, tiles)),
            dma((2, shards, groups * tiles)),
            dma((2, shards, groups * tiles)),
        ],
        compiler_params=pltpu.CompilerParams(
            collective_id=0, has_side_effects=True, vmem_limit_bytes=40 * 2**20
        ),
    )(step, x, master, one, two, average)


def body(sizes, limit, qkv_grad, master, moment_one, moment_two, average, step):
    shards, groups, _ = sizes
    rows = qkv_grad.shape[1] // (shards * groups)
    cols = qkv_grad.shape[2]
    weights, new_master, new_one, new_two, new_average = adam_step(
        sizes,
        limit,
        step.reshape(1),
        qkv_grad.reshape(shards, groups, rows, cols),
        master,
        moment_one,
        moment_two,
        average.reshape(groups, rows, cols),
    )
    return (
        weights.reshape(shards * groups * rows, cols),
        new_master,
        new_one,
        new_two,
        new_average.reshape(average.shape),
    )


def solution(mesh):
    state = P(("section", "shard", "tensor"), None)
    in_specs = (
        P("shard", "section", "tensor"),
        state,
        state,
        state,
        P(("section", "shard"), "tensor"),
        P(),
    )
    out_specs = (
        P("section", "tensor"),
        state,
        state,
        state,
        P(("section", "shard"), "tensor"),
    )
    sizes = tuple(mesh.shape[name] for name in ("shard", "tensor", "section"))

    def run(qkv_grad, master, moment_one, moment_two, average, step):
        limit = math.sqrt(master.shape[0] * master.shape[1])
        fn = functools.partial(body, sizes, limit)
        return jax.shard_map(fn, mesh=mesh, in_specs=in_specs, out_specs=out_specs, check_vma=False)(
            qkv_grad, master, moment_one, moment_two, average, step
        )

    return run
```

```python
import functools
import math

import jax
import jax.numpy as jnp
from jax import lax
from jax.experimental import pallas as pl
from jax.experimental.pallas import tpu as pltpu
from jax.sharding import PartitionSpec as P

MESH = pl.DeviceIdType.MESH
DEPTH = 6
LAG = 2


def step_kernel(
    sizes, limit, step, x, master, one, two, average,
    w_low, w_high, out_master, out_one, out_two, out_average,
    held, inbox, gbox, half, square, zbox, pbox,
    x_sem, state_sem, hop_send, hop_recv, sum_send, sum_recv, z_send, z_recv, p_send, p_recv,
    y_send, y_recv, out_send, out_recv,
):
    shards, groups, sections = sizes
    s, t, c = lax.axis_index("shard"), lax.axis_index("tensor"), lax.axis_index("section")
    last = shards - 1
    near = shards // 2
    _, _, rows, cols = x.shape
    tile = inbox.shape[2]
    tiles = rows // tile
    share = groups * tiles
    count = near * share
    plane = groups * sections
    depth = max(DEPTH, groups)
    at_end = jnp.logical_or(s == 0, s == last)
    end = jnp.minimum(s, 1)

    def load(q, g):
        return pltpu.make_async_copy(x.at[q, g], held.at[q, g], x_sem.at[q, g])

    def fetch(n):
        for g in range(groups):
            @pl.when(s > 0)
            def _():
                load(near + n, g).start()

            @pl.when(s < last)
            def _():
                load(near - 1 - n, g).start()

    states = [
        pltpu.make_async_copy(src, dst, state_sem.at[n])
        for n, (src, dst) in enumerate(
            ((master, out_master), (one, out_one), (two, out_two), (average, out_average))
        )
    ]

    barrier = pltpu.get_barrier_semaphore()

    def peer(off):
        at = lax.rem(t * sections + c + off, plane)
        return {"tensor": lax.div(at, sections), "section": lax.rem(at, sections)}

    @pl.loop(1, plane)
    def _(off):
        pl.semaphore_signal(barrier, inc=1, device_id=peer(off), device_id_type=MESH)

    @pl.loop(groups, shards * groups)
    def _(off):
        pl.semaphore_signal(
            barrier,
            inc=1,
            device_id={
                "shard": lax.rem(s + lax.div(off, groups), shards),
                "tensor": lax.rem(t + lax.rem(off, groups), groups),
            },
            device_id_type=MESH,
        )

    fetch(0)
    square[...] = jnp.zeros_like(square)
    zbox[...] = jnp.zeros_like(zbox)
    pl.semaphore_wait(barrier, plane - 1 + (shards - 1) * groups)

    def place(way, i):
        n, rest = lax.div(i, share), lax.rem(i, share)
        j, g = lax.div(rest, groups), lax.rem(rest, groups)
        return (near + n if way == 0 else near - 1 - n), g, j

    def part(j):
        return pl.ds(pl.multiple_of(j * tile, tile), tile)

    def hop(way, i, src):
        return pltpu.make_async_remote_copy(
            src_ref=src,
            dst_ref=inbox.at[way, i],
            send_sem=hop_send.at[way, i],
            recv_sem=hop_recv.at[way, i],
            device_id={"shard": jnp.minimum(s + 1, last) if way == 0 else jnp.maximum(s - 1, 0)},
            device_id_type=MESH,
        )

    def hand(way, i):
        q, g, j = place(way, i)
        return pltpu.make_async_remote_copy(
            src_ref=inbox.at[way, i],
            dst_ref=gbox.at[t, part(j)],
            send_sem=sum_send.at[i],
            recv_sem=sum_recv.at[t, j],
            device_id={"shard": q, "tensor": g},
            device_id_type=MESH,
        )

    def summed(g, j):
        return pltpu.make_async_remote_copy(
            src_ref=gbox.at[g, part(j)],
            dst_ref=gbox.at[g, part(j)],
            send_sem=sum_send.at[0],
            recv_sem=sum_recv.at[g, j],
            device_id={"tensor": g},
            device_id_type=MESH,
        )

    @pl.loop(0, count + LAG * last)
    def _(now):
        @pl.when(now == 1)
        def _():
            for n in range(1, near):
                fetch(n)

        @pl.when(now == LAG * last)
        def _():
            for copy in states:
                copy.start()

        for way in (0, 1):
            lag = s if way == 0 else last - s
            i = now - LAG * lag
            q, g, j = place(way, i)

            @pl.when(jnp.logical_and(i >= 0, i < count))
            def _():
                @pl.when(jnp.logical_and(lag < last, i >= DEPTH))
                def _():
                    hop(way, i - DEPTH, inbox.at[way, i - DEPTH]).wait_send()

                @pl.when(lag == 0)
                def _():
                    hop(way, i, x.at[q, g, part(j)]).start()

                @pl.when(lag > 0)
                def _():
                    @pl.when(j == 0)
                    def _():
                        load(q, g).wait()

                    hop(way, i, inbox.at[way, i]).wait_recv()
                    acc = inbox[way, i].astype(jnp.float32) + held[q, g, part(j)].astype(jnp.float32)
                    short = acc.astype(jnp.bfloat16)

                    @pl.when(lag < last)
                    def _():
                        inbox[way, i] = short
                        hop(way, i, inbox.at[way, i]).start()

                    @pl.when(lag == last)
                    def _():
                        square[...] += jnp.sum((acc * acc).reshape(tile // 8, 8, cols), axis=0)
                        mine = jnp.logical_and(q == s, g == t)

                        @pl.when(mine)
                        def _():
                            gbox[t, part(j)] = short

                        @pl.when(jnp.logical_not(mine))
                        def _():
                            inbox[way, i] = short

                        @pl.when(jnp.logical_and(q == s, g != t))
                        def _():
                            hand(way, i).start()

    def spread(off):
        return pltpu.make_async_remote_copy(
            src_ref=zbox.at[end],
            dst_ref=zbox.at[end],
            send_sem=z_send.at[off],
            recv_sem=z_recv.at[end],
            device_id={"shard": lax.rem(s + off, shards)},
            device_id_type=MESH,
        )

    def level(off):
        return pltpu.make_async_remote_copy(
            src_ref=pbox.at[0],
            dst_ref=pbox.at[off],
            send_sem=p_send.at[off],
            recv_sem=p_recv.at[off],
            device_id=peer(off),
            device_id_type=MESH,
        )

    def came(slot):
        return pltpu.make_async_copy(zbox.at[slot], zbox.at[slot], z_recv.at[slot])

    @pl.when(at_end)
    def _():
        narrow = square[:, :128]
        for n in range(1, cols // 128):
            narrow = narrow + square[:, n * 128 : (n + 1) * 128]
        zbox[end] = narrow

        @pl.loop(1, shards)
        def _(off):
            spread(off).start()

    for way, where in ((0, last), (1, 0)):
        @pl.when(s == where)
        def _():
            @pl.loop(0, count - share)
            def _(i):
                hand(way, i).start()

    @pl.when(s > 0)
    def _():
        came(0).wait()

    @pl.when(s < last)
    def _():
        came(1).wait()

    pbox[0] = zbox[0] + zbox[1]

    @pl.loop(1, plane)
    def _(off):
        level(off).start()

    for way, here in ((0, s < last), (1, s > 0)):
        @pl.when(here)
        def _():
            @pl.loop(max(count - DEPTH, 0), count)
            def _(i):
                hop(way, i, inbox.at[way, i]).wait_send()

    for copy in states:
        copy.wait()
    times = jnp.full((8, 128), step[0].astype(jnp.float32))
    first_fix = jnp.max(1.0 / (1.0 - jnp.exp(times * math.log(0.9))))
    second_fix = jnp.max(1.0 / (1.0 - jnp.exp(times * math.log(0.95))))

    @pl.loop(1, plane)
    def _(off):
        level(off).wait_recv()

    whole = pbox[0]
    for n in range(1, plane):
        whole = whole + pbox[n]
    norm = jnp.sqrt(jnp.full((8, 128), jnp.sum(whole)))
    clip = jnp.max(jnp.minimum(1.0, limit / (norm + 1e-06)))

    def within(p, use):
        @pl.when(p < near)
        def _():
            use(w_low, p)

        @pl.when(p >= near)
        def _():
            use(w_high, p - near)

    def cross(k, j, w=w_low, row=0):
        return pltpu.make_async_remote_copy(
            src_ref=half.at[k, part(j)],
            dst_ref=w.at[row, t, part(j)],
            send_sem=y_send.at[k, j],
            recv_sem=y_recv.at[k, j],
            device_id={"tensor": lax.rem(t + k, groups)},
            device_id_type=MESH,
        )

    def crossed(k, j):
        g = lax.rem(t + k, groups)
        return pltpu.make_async_remote_copy(
            src_ref=w_low.at[0, g, part(j)],
            dst_ref=w_low.at[0, g, part(j)],
            send_sem=y_send.at[k, j],
            recv_sem=y_recv.at[groups - k, j],
            device_id={"tensor": g},
            device_id_type=MESH,
        )

    def source(way, n):
        away = lax.div(n, share)
        return s - away if way == 0 else s + away

    def forward(way, n, w=w_low, row=0):
        m = lax.rem(n, share)
        p = source(way, n)
        j, k = lax.div(m, groups), lax.rem(m, groups)
        block = w.at[row, lax.rem(t + k, groups), part(j)]
        return pltpu.make_async_remote_copy(
            src_ref=block,
            dst_ref=block,
            send_sem=out_send.at[way, p, m],
            recv_sem=out_recv.at[way, p, m],
            device_id={"shard": jnp.minimum(s + 1, last) if way == 0 else jnp.maximum(s - 1, 0)},
            device_id_type=MESH,
        )

    def ways(n, wait, here=True):
        for way in (0, 1):
            reach = s if way == 0 else last - s

            @pl.when(jnp.logical_and(n < (reach + 1) * share, here))
            def _():
                if wait:
                    forward(way, n).wait_recv()

                @pl.when(s < last if way == 0 else s > 0)
                def _():
                    @pl.when(n >= depth)
                    def _():
                        forward(way, n - depth).wait_send()

                    within(source(way, n), lambda w, row: forward(way, n, w, row).start())

    @pl.loop(0, share + groups)
    def _(now):
        j, k = lax.div(now, groups), lax.rem(now, groups)
        g = lax.rem(t + k, groups)

        @pl.when(now < share)
        def _():
            there = pl.ds(pl.multiple_of(g * cols, 128), cols)

            @pl.when(jnp.logical_not(jnp.logical_and(at_end, k == 0)))
            def _():
                summed(g, j).wait_recv()

            clipped = clip * gbox[g, part(j)].astype(jnp.float32)
            new_one = 0.9 * out_one[part(j), there] + 0.1 * clipped
            new_two = 0.95 * out_two[part(j), there] + 0.05 * clipped * clipped
            update = new_one * first_fix / (jnp.sqrt(new_two * second_fix) + 1e-08)
            new_master = out_master[part(j), there] * (1.0 - 0.1 * 0.1) - 0.1 * update
            out_one[part(j), there] = new_one
            out_two[part(j), there] = new_two
            out_master[part(j), there] = new_master
            short = new_master.astype(jnp.bfloat16)

            @pl.when(k == 0)
            def _():
                def keep(w, row):
                    w[row, t, part(j)] = short

                within(s, keep)
                ways(now, False)

            @pl.when(k > 0)
            def _():
                half[k, part(j)] = short
                within(s, lambda w, row: cross(k, j, w, row).start())

        @pl.when(jnp.logical_and(k > 0, now >= groups))
        def _():
            crossed(k, j - 1).wait_recv()
            ways(now - groups, False)

    @pl.loop(share, shards * share)
    def _(n):
        m = n - share
        ways(n, True)

        @pl.when(m < share)
        def _():
            j, g = lax.div(m, groups), lax.rem(m, groups)

            def mix(w, row):
                fresh = w[row, g, part(j)].astype(jnp.float32)
                out_average[g, part(j)] = 0.99 * out_average[g, part(j)] + 0.01 * fresh

            within(s, mix)

    for way in (0, 1):
        reach = s if way == 0 else last - s

        @pl.when(s < last if way == 0 else s > 0)
        def _():
            @pl.loop(0, depth)
            def _(n):
                left = (reach + 1) * share - 1 - n

                @pl.when(left >= 0)
                def _():
                    forward(way, left).wait_send()

    for k in range(1, groups):
        @pl.loop(0, tiles)
        def _(j):
            cross(k, j).wait_send()

    for way, where in ((0, last), (1, 0)):
        @pl.when(s == where)
        def _():
            @pl.loop(0, count)
            def _(i):
                q, g, _ = place(way, i)

                @pl.when(jnp.logical_not(jnp.logical_and(q == s, g == t)))
                def _():
                    hand(way, i).wait_send()

    @pl.when(at_end)
    def _():
        @pl.loop(1, shards)
        def _(off):
            spread(off).wait_send()

    @pl.loop(1, plane)
    def _(off):
        level(off).wait_send()


def adam_step(sizes, limit, step, x, master, one, two, average):
    shards, groups, sections = sizes
    _, _, rows, cols = x.shape
    tile = min(rows, 16)
    tiles = rows // tile
    count = shards // 2 * groups * tiles
    plane = groups * sections
    dma = pltpu.SemaphoreType.DMA
    anywhere = pl.BlockSpec(memory_space=pl.ANY)
    near = pl.BlockSpec(memory_space=pltpu.VMEM)
    state = jax.ShapeDtypeStruct(master.shape, jnp.float32)
    weights = jax.ShapeDtypeStruct((shards // 2,) + x.shape[1:], jnp.bfloat16)
    return pl.pallas_call(
        functools.partial(step_kernel, sizes, limit),
        out_shape=[
            weights,
            weights,
            state,
            state,
            state,
            jax.ShapeDtypeStruct(average.shape, jnp.float32),
        ],
        in_specs=[pl.BlockSpec(memory_space=pltpu.SMEM)] + [anywhere] * 5,
        out_specs=[near] * 6,
        scratch_shapes=[
            pltpu.VMEM(x.shape, jnp.bfloat16),
            pltpu.VMEM((2, count, tile, cols), jnp.bfloat16),
            pltpu.VMEM((groups, rows, cols), jnp.bfloat16),
            pltpu.VMEM((groups, rows, cols), jnp.bfloat16),
            pltpu.VMEM((8, cols), jnp.float32),
            pltpu.VMEM((2, 8, 128), jnp.float32),
            pltpu.VMEM((plane, 8, 128), jnp.float32),
            dma((shards, groups)),
            dma((4,)),
            dma((2, count)),
            dma((2, count)),
            dma((count,)),
            dma((groups, tiles)),
            dma((shards,)),
            dma((2,)),
            dma((plane,)),
            dma((plane,)),
            dma((groups, tiles)),
            dma((groups, tiles)),
            dma((2, shards, groups * tiles)),
            dma((2, shards, groups * tiles)),
        ],
        compiler_params=pltpu.CompilerParams(
            collective_id=0, has_side_effects=True, vmem_limit_bytes=34 * 2**20
        ),
    )(step, x, master, one, two, average)


def store_kernel(low, high, master, one, two, average, w, *rest):
    outs, sem = rest[:-1], rest[-1]
    half = low.shape[0]
    pairs = [(low, w.at[pl.ds(0, half)]), (high, w.at[pl.ds(half, half)])]
    pairs += zip((master, one, two, average), outs)
    copies = [pltpu.make_async_copy(src, dst, sem.at[n]) for n, (src, dst) in enumerate(pairs)]
    for copy in copies:
        copy.start()
    for copy in copies:
        copy.wait()


def store(low, high, *arrays):
    shape = (2 * low.shape[0],) + low.shape[1:]
    return pl.pallas_call(
        store_kernel,
        out_shape=[jax.ShapeDtypeStruct(shape, low.dtype)]
        + [jax.ShapeDtypeStruct(a.shape, a.dtype) for a in arrays],
        in_specs=[pl.BlockSpec(memory_space=pltpu.VMEM)] * (len(arrays) + 2),
        out_specs=[pl.BlockSpec(memory_space=pl.ANY)] * (len(arrays) + 1),
        scratch_shapes=[pltpu.SemaphoreType.DMA((len(arrays) + 2,))],
        compiler_params=pltpu.CompilerParams(vmem_limit_bytes=34 * 2**20),
    )(low, high, *arrays)


def body(sizes, limit, qkv_grad, master, moment_one, moment_two, average, step):
    shards, groups, _ = sizes
    rows = qkv_grad.shape[1] // (shards * groups)
    cols = qkv_grad.shape[2]
    parts = adam_step(
        sizes,
        limit,
        step.reshape(1),
        qkv_grad.reshape(shards, groups, rows, cols),
        master,
        moment_one,
        moment_two,
        average.reshape(groups, rows, cols),
    )
    weights, new_master, new_one, new_two, new_average = store(*parts)
    return (
        weights.reshape(shards * groups * rows, cols),
        new_master,
        new_one,
        new_two,
        new_average.reshape(average.shape),
    )


def solution(mesh):
    state = P(("section", "shard", "tensor"), None)
    in_specs = (
        P("shard", "section", "tensor"),
        state,
        state,
        state,
        P(("section", "shard"), "tensor"),
        P(),
    )
    out_specs = (
        P("section", "tensor"),
        state,
        state,
        state,
        P(("section", "shard"), "tensor"),
    )
    sizes = tuple(mesh.shape[name] for name in ("shard", "tensor", "section"))

    def run(qkv_grad, master, moment_one, moment_two, average, step):
        limit = math.sqrt(master.shape[0] * master.shape[1])
        fn = functools.partial(body, sizes, limit)
        return jax.shard_map(fn, mesh=mesh, in_specs=in_specs, out_specs=out_specs, check_vma=False)(
            qkv_grad, master, moment_one, moment_two, average, step
        )

    return run
```

```python
import functools
import math

import jax
import jax.numpy as jnp
from jax import lax
from jax.experimental import pallas as pl
from jax.experimental.pallas import tpu as pltpu
from jax.sharding import PartitionSpec as P

MESH = pl.DeviceIdType.MESH
DEPTH = 6
LAG = 2
KEPT = 1


def step_kernel(
    sizes, limit, step, x, master, one, two, average,
    w_low, w_high, out_master, out_one, out_two, out_average,
    held, inbox, gbox, half, extra, square, zbox, pbox,
    x_sem, state_sem, hop_send, hop_recv, extra_send, extra_recv, sum_send, sum_recv, z_send, z_recv, p_send, p_recv,
    y_send, y_recv, out_send, out_recv,
):
    shards, groups, sections = sizes
    s, t, c = lax.axis_index("shard"), lax.axis_index("tensor"), lax.axis_index("section")
    last = shards - 1
    near = shards // 2
    _, _, rows, cols = x.shape
    tile = inbox.shape[2]
    tiles = rows // tile
    share = groups * tiles
    count = near * share
    plane = groups * sections
    depth = max(DEPTH, groups)
    at_end = jnp.logical_or(s == 0, s == last)
    at_near = jnp.logical_or(s == 1, s == last - 1)
    kept = split(shards, tiles)
    holders = [0, last] + ([1, last - 1] if kept else [])

    def load(q, g):
        return pltpu.make_async_copy(x.at[q, g], held.at[q, g], x_sem.at[q, g])

    def fetch(n):
        for g in range(groups):
            @pl.when(s > 0)
            def _():
                load(last - n, g).start()

            @pl.when(s < last)
            def _():
                load(n, g).start()

    states = [
        pltpu.make_async_copy(src, dst, state_sem.at[n])
        for n, (src, dst) in enumerate(
            ((master, out_master), (one, out_one), (two, out_two), (average, out_average))
        )
    ]

    barrier = pltpu.get_barrier_semaphore()

    def peer(off):
        at = lax.rem(t * sections + c + off, plane)
        return {"tensor": lax.div(at, sections), "section": lax.rem(at, sections)}

    @pl.loop(1, plane)
    def _(off):
        pl.semaphore_signal(barrier, inc=1, device_id=peer(off), device_id_type=MESH)

    @pl.loop(groups, shards * groups)
    def _(off):
        pl.semaphore_signal(
            barrier,
            inc=1,
            device_id={
                "shard": lax.rem(s + lax.div(off, groups), shards),
                "tensor": lax.rem(t + lax.rem(off, groups), groups),
            },
            device_id_type=MESH,
        )

    fetch(0)
    square[...] = jnp.zeros_like(square)
    zbox[...] = jnp.zeros_like(zbox)
    pl.semaphore_wait(barrier, plane - 1 + (shards - 1) * groups)

    def place(way, i):
        n, rest = lax.div(i, share), lax.rem(i, share)
        j, g = lax.div(rest, groups), lax.rem(rest, groups)
        return (last - n if way == 0 else n), g, j

    def short_of(way, q, j):
        return jnp.logical_and(q == (last - 1 if way == 0 else 1), j >= tiles - kept)

    def part(j):
        return pl.ds(pl.multiple_of(j * tile, tile), tile)

    def hop(way, i, src):
        return pltpu.make_async_remote_copy(
            src_ref=src,
            dst_ref=inbox.at[way, i],
            send_sem=hop_send.at[way, i],
            recv_sem=hop_recv.at[way, i],
            device_id={"shard": jnp.minimum(s + 1, last) if way == 0 else jnp.maximum(s - 1, 0)},
            device_id_type=MESH,
        )

    def spare(g, j, q=0):
        e = (j - (tiles - kept)) * groups + g
        return pltpu.make_async_remote_copy(
            src_ref=x.at[q, g, part(j)],
            dst_ref=extra.at[e],
            send_sem=extra_send.at[e],
            recv_sem=extra_recv.at[e],
            device_id={"shard": jnp.where(s == 0, 1, last - 1)},
            device_id_type=MESH,
        )

    def spares(use):
        for q, where in ((1, 0), (last - 1, last)):
            @pl.when(s == where)
            def _():
                for j in range(tiles - kept, tiles):
                    for g in range(groups):
                        use(spare(g, j, q))

    def hand(way, i):
        q, g, j = place(way, i)
        return pltpu.make_async_remote_copy(
            src_ref=inbox.at[way, i],
            dst_ref=gbox.at[t, part(j)],
            send_sem=sum_send.at[i],
            recv_sem=sum_recv.at[t, j],
            device_id={"shard": q, "tensor": g},
            device_id_type=MESH,
        )

    def summed(g, j):
        return pltpu.make_async_remote_copy(
            src_ref=gbox.at[g, part(j)],
            dst_ref=gbox.at[g, part(j)],
            send_sem=sum_send.at[0],
            recv_sem=sum_recv.at[g, j],
            device_id={"tensor": g},
            device_id_type=MESH,
        )

    @pl.loop(0, count + LAG * last)
    def _(now):
        @pl.when(now == 1)
        def _():
            for n in range(1, near):
                fetch(n)

        @pl.when(now == LAG * last)
        def _():
            for copy in states:
                copy.start()

        for way in (0, 1):
            lag = s if way == 0 else last - s
            i = now - LAG * lag
            q, g, j = place(way, i)
            cut = short_of(way, q, j)
            stop = jnp.where(cut, last - 1, last)

            def finish(acc):
                short = acc.astype(jnp.bfloat16)
                square[...] += jnp.sum((acc * acc).reshape(tile // 8, 8, cols), axis=0)
                mine = jnp.logical_and(q == s, g == t)

                @pl.when(mine)
                def _():
                    gbox[t, part(j)] = short

                @pl.when(jnp.logical_not(mine))
                def _():
                    inbox[way, i] = short

                @pl.when(jnp.logical_and(q == s, g != t))
                def _():
                    hand(way, i).start()

            @pl.when(jnp.logical_and(jnp.logical_and(i >= 0, i < count), lag <= stop))
            def _():
                before_q, _, before_j = place(way, i - DEPTH)
                before_cut = short_of(way, before_q, before_j)
                before_stop = jnp.where(before_cut, last - 1, last)

                @pl.when(jnp.logical_and(lag < before_stop, i >= DEPTH))
                def _():
                    hop(way, i - DEPTH, inbox.at[way, i - DEPTH]).wait_send()

                @pl.when(lag == 0)
                def _():
                    hop(way, i, x.at[q, g, part(j)]).start()

                @pl.when(lag > 0)
                def _():
                    @pl.when(j == 0)
                    def _():
                        load(q, g).wait()

                    hop(way, i, inbox.at[way, i]).wait_recv()
                    acc = inbox[way, i].astype(jnp.float32) + held[q, g, part(j)].astype(jnp.float32)

                    @pl.when(lag < stop)
                    def _():
                        inbox[way, i] = acc.astype(jnp.bfloat16)
                        hop(way, i, inbox.at[way, i]).start()

                    @pl.when(jnp.logical_and(lag == stop, jnp.logical_not(cut)))
                    def _():
                        finish(acc)

                    if kept:
                        @pl.when(jnp.logical_and(lag == stop, cut))
                        def _():
                            spare(g, j).wait_recv()
                            e = (j - (tiles - kept)) * groups + g
                            finish(acc + extra[e].astype(jnp.float32))

        if kept:
            @pl.when(now == count - 1)
            def _():
                spares(lambda copy: copy.start())

    def spread(off):
        return pltpu.make_async_remote_copy(
            src_ref=zbox.at[s],
            dst_ref=zbox.at[s],
            send_sem=z_send.at[off],
            recv_sem=z_recv.at[s],
            device_id={"shard": lax.rem(s + off, shards)},
            device_id_type=MESH,
        )

    def level(off):
        return pltpu.make_async_remote_copy(
            src_ref=pbox.at[0],
            dst_ref=pbox.at[off],
            send_sem=p_send.at[off],
            recv_sem=p_recv.at[off],
            device_id=peer(off),
            device_id_type=MESH,
        )

    def came(slot):
        return pltpu.make_async_copy(zbox.at[slot], zbox.at[slot], z_recv.at[slot])

    holding = jnp.logical_or(at_end, at_near) if kept else at_end

    @pl.when(holding)
    def _():
        narrow = square[:, :128]
        for n in range(1, cols // 128):
            narrow = narrow + square[:, n * 128 : (n + 1) * 128]
        zbox[s] = narrow

        @pl.loop(1, shards)
        def _(off):
            spread(off).start()

    for way, where in ((0, last), (1, 0)):
        @pl.when(s == where)
        def _():
            @pl.loop(share, count)
            def _(i):
                q, _, j = place(way, i)

                @pl.when(jnp.logical_not(short_of(way, q, j)))
                def _():
                    hand(way, i).start()

    for holder in holders:
        @pl.when(s != holder)
        def _():
            came(holder).wait()

    total = zbox[holders[0]]
    for holder in holders[1:]:
        total = total + zbox[holder]
    pbox[0] = total

    @pl.loop(1, plane)
    def _(off):
        level(off).start()

    for way, here in ((0, s < last), (1, s > 0)):
        @pl.when(here)
        def _():
            @pl.loop(max(count - DEPTH, 0), count)
            def _(i):
                q, _, j = place(way, i)
                lag = s if way == 0 else last - s

                @pl.when(lag < jnp.where(short_of(way, q, j), last - 1, last))
                def _():
                    hop(way, i, inbox.at[way, i]).wait_send()

    for copy in states:
        copy.wait()
    times = jnp.full((8, 128), step[0].astype(jnp.float32))
    first_fix = jnp.max(1.0 / (1.0 - jnp.exp(times * math.log(0.9))))
    second_fix = jnp.max(1.0 / (1.0 - jnp.exp(times * math.log(0.95))))

    @pl.loop(1, plane)
    def _(off):
        level(off).wait_recv()

    whole = pbox[0]
    for n in range(1, plane):
        whole = whole + pbox[n]
    norm = jnp.sqrt(jnp.full((8, 128), jnp.sum(whole)))
    clip = jnp.max(jnp.minimum(1.0, limit / (norm + 1e-06)))

    def within(p, use):
        @pl.when(p < near)
        def _():
            use(w_low, p)

        @pl.when(p >= near)
        def _():
            use(w_high, p - near)

    def cross(k, j, w=w_low, row=0):
        return pltpu.make_async_remote_copy(
            src_ref=half.at[k, part(j)],
            dst_ref=w.at[row, t, part(j)],
            send_sem=y_send.at[k, j],
            recv_sem=y_recv.at[k, j],
            device_id={"tensor": lax.rem(t + k, groups)},
            device_id_type=MESH,
        )

    def crossed(k, j):
        g = lax.rem(t + k, groups)
        return pltpu.make_async_remote_copy(
            src_ref=w_low.at[0, g, part(j)],
            dst_ref=w_low.at[0, g, part(j)],
            send_sem=y_send.at[k, j],
            recv_sem=y_recv.at[groups - k, j],
            device_id={"tensor": g},
            device_id_type=MESH,
        )

    def source(way, n):
        away = lax.div(n, share)
        return s - away if way == 0 else s + away

    def forward(way, n, w=w_low, row=0):
        m = lax.rem(n, share)
        p = source(way, n)
        j, k = lax.div(m, groups), lax.rem(m, groups)
        block = w.at[row, lax.rem(t + k, groups), part(j)]
        return pltpu.make_async_remote_copy(
            src_ref=block,
            dst_ref=block,
            send_sem=out_send.at[way, p, m],
            recv_sem=out_recv.at[way, p, m],
            device_id={"shard": jnp.minimum(s + 1, last) if way == 0 else jnp.maximum(s - 1, 0)},
            device_id_type=MESH,
        )

    def ways(n, wait, here=True):
        for way in (0, 1):
            reach = s if way == 0 else last - s

            @pl.when(jnp.logical_and(n < (reach + 1) * share, here))
            def _():
                if wait:
                    forward(way, n).wait_recv()

                @pl.when(s < last if way == 0 else s > 0)
                def _():
                    @pl.when(n >= depth)
                    def _():
                        forward(way, n - depth).wait_send()

                    within(source(way, n), lambda w, row: forward(way, n, w, row).start())

    @pl.loop(0, share + groups)
    def _(now):
        j, k = lax.div(now, groups), lax.rem(now, groups)
        g = lax.rem(t + k, groups)

        @pl.when(now < share)
        def _():
            there = pl.ds(pl.multiple_of(g * cols, 128), cols)

            local = jnp.logical_or(at_end, jnp.logical_and(at_near, j >= tiles - kept)) if kept else at_end

            @pl.when(jnp.logical_not(jnp.logical_and(local, k == 0)))
            def _():
                summed(g, j).wait_recv()

            clipped = clip * gbox[g, part(j)].astype(jnp.float32)
            new_one = 0.9 * out_one[part(j), there] + 0.1 * clipped
            new_two = 0.95 * out_two[part(j), there] + 0.05 * clipped * clipped
            update = new_one * first_fix / (jnp.sqrt(new_two * second_fix) + 1e-08)
            new_master = out_master[part(j), there] * (1.0 - 0.1 * 0.1) - 0.1 * update
            out_one[part(j), there] = new_one
            out_two[part(j), there] = new_two
            out_master[part(j), there] = new_master
            short = new_master.astype(jnp.bfloat16)

            @pl.when(k == 0)
            def _():
                def keep(w, row):
                    w[row, t, part(j)] = short

                within(s, keep)
                ways(now, False)

            @pl.when(k > 0)
            def _():
                half[k, part(j)] = short
                within(s, lambda w, row: cross(k, j, w, row).start())

        @pl.when(jnp.logical_and(k > 0, now >= groups))
        def _():
            crossed(k, j - 1).wait_recv()
            ways(now - groups, False)

    @pl.loop(share, shards * share)
    def _(n):
        m = n - share
        ways(n, True)

        @pl.when(m < share)
        def _():
            j, g = lax.div(m, groups), lax.rem(m, groups)

            def mix(w, row):
                fresh = w[row, g, part(j)].astype(jnp.float32)
                out_average[g, part(j)] = 0.99 * out_average[g, part(j)] + 0.01 * fresh

            within(s, mix)

    for way in (0, 1):
        reach = s if way == 0 else last - s

        @pl.when(s < last if way == 0 else s > 0)
        def _():
            @pl.loop(0, depth)
            def _(n):
                left = (reach + 1) * share - 1 - n

                @pl.when(left >= 0)
                def _():
                    forward(way, left).wait_send()

    for k in range(1, groups):
        @pl.loop(0, tiles)
        def _(j):
            cross(k, j).wait_send()

    for way in (0, 1):
        @pl.when(s >= near if way == 0 else s < near)
        def _():
            @pl.loop(0, count)
            def _(i):
                q, g, j = place(way, i)
                cut = short_of(way, q, j)
                here = jnp.logical_or(
                    jnp.logical_and(at_end, jnp.logical_not(cut)), jnp.logical_and(q == s, cut)
                )

                @pl.when(jnp.logical_and(here, jnp.logical_not(jnp.logical_and(q == s, g == t))))
                def _():
                    hand(way, i).wait_send()

    if kept:
        spares(lambda copy: copy.wait_send())

    @pl.when(holding)
    def _():
        @pl.loop(1, shards)
        def _(off):
            spread(off).wait_send()

    @pl.loop(1, plane)
    def _(off):
        level(off).wait_send()


def split(shards, tiles):
    return KEPT if shards >= 4 and tiles > KEPT else 0


def adam_step(sizes, limit, step, x, master, one, two, average):
    shards, groups, sections = sizes
    _, _, rows, cols = x.shape
    tile = min(rows, 16)
    tiles = rows // tile
    count = shards // 2 * groups * tiles
    plane = groups * sections
    dma = pltpu.SemaphoreType.DMA
    anywhere = pl.BlockSpec(memory_space=pl.ANY)
    near = pl.BlockSpec(memory_space=pltpu.VMEM)
    state = jax.ShapeDtypeStruct(master.shape, jnp.float32)
    weights = jax.ShapeDtypeStruct((shards // 2,) + x.shape[1:], jnp.bfloat16)
    return pl.pallas_call(
        functools.partial(step_kernel, sizes, limit),
        out_shape=[
            weights,
            weights,
            state,
            state,
            state,
            jax.ShapeDtypeStruct(average.shape, jnp.float32),
        ],
        in_specs=[pl.BlockSpec(memory_space=pltpu.SMEM)] + [anywhere] * 5,
        out_specs=[near] * 6,
        scratch_shapes=[
            pltpu.VMEM(x.shape, jnp.bfloat16),
            pltpu.VMEM((2, count, tile, cols), jnp.bfloat16),
            pltpu.VMEM((groups, rows, cols), jnp.bfloat16),
            pltpu.VMEM((groups, rows, cols), jnp.bfloat16),
            pltpu.VMEM((max(split(shards, tiles), 1) * groups, tile, cols), jnp.bfloat16),
            pltpu.VMEM((8, cols), jnp.float32),
            pltpu.VMEM((shards, 8, 128), jnp.float32),
            pltpu.VMEM((plane, 8, 128), jnp.float32),
            dma((shards, groups)),
            dma((4,)),
            dma((2, count)),
            dma((2, count)),
            dma((max(split(shards, tiles), 1) * groups,)),
            dma((max(split(shards, tiles), 1) * groups,)),
            dma((count,)),
            dma((groups, tiles)),
            dma((shards,)),
            dma((shards,)),
            dma((plane,)),
            dma((plane,)),
            dma((groups, tiles)),
            dma((groups, tiles)),
            dma((2, shards, groups * tiles)),
            dma((2, shards, groups * tiles)),
        ],
        compiler_params=pltpu.CompilerParams(
            collective_id=0, has_side_effects=True, vmem_limit_bytes=34 * 2**20
        ),
    )(step, x, master, one, two, average)


def store_kernel(low, high, master, one, two, average, w, *rest):
    outs, sem = rest[:-1], rest[-1]
    half = low.shape[0]
    pairs = [(low, w.at[pl.ds(0, half)]), (high, w.at[pl.ds(half, half)])]
    pairs += zip((master, one, two, average), outs)
    copies = [pltpu.make_async_copy(src, dst, sem.at[n]) for n, (src, dst) in enumerate(pairs)]
    for copy in copies:
        copy.start()
    for copy in copies:
        copy.wait()


def store(low, high, *arrays):
    shape = (2 * low.shape[0],) + low.shape[1:]
    return pl.pallas_call(
        store_kernel,
        out_shape=[jax.ShapeDtypeStruct(shape, low.dtype)]
        + [jax.ShapeDtypeStruct(a.shape, a.dtype) for a in arrays],
        in_specs=[pl.BlockSpec(memory_space=pltpu.VMEM)] * (len(arrays) + 2),
        out_specs=[pl.BlockSpec(memory_space=pl.ANY)] * (len(arrays) + 1),
        scratch_shapes=[pltpu.SemaphoreType.DMA((len(arrays) + 2,))],
        compiler_params=pltpu.CompilerParams(vmem_limit_bytes=34 * 2**20),
    )(low, high, *arrays)


def body(sizes, limit, qkv_grad, master, moment_one, moment_two, average, step):
    shards, groups, _ = sizes
    rows = qkv_grad.shape[1] // (shards * groups)
    cols = qkv_grad.shape[2]
    parts = adam_step(
        sizes,
        limit,
        step.reshape(1),
        qkv_grad.reshape(shards, groups, rows, cols),
        master,
        moment_one,
        moment_two,
        average.reshape(groups, rows, cols),
    )
    weights, new_master, new_one, new_two, new_average = store(*parts)
    return (
        weights.reshape(shards * groups * rows, cols),
        new_master,
        new_one,
        new_two,
        new_average.reshape(average.shape),
    )


def solution(mesh):
    state = P(("section", "shard", "tensor"), None)
    in_specs = (
        P("shard", "section", "tensor"),
        state,
        state,
        state,
        P(("section", "shard"), "tensor"),
        P(),
    )
    out_specs = (
        P("section", "tensor"),
        state,
        state,
        state,
        P(("section", "shard"), "tensor"),
    )
    sizes = tuple(mesh.shape[name] for name in ("shard", "tensor", "section"))

    def run(qkv_grad, master, moment_one, moment_two, average, step):
        limit = math.sqrt(master.shape[0] * master.shape[1])
        fn = functools.partial(body, sizes, limit)
        return jax.shard_map(fn, mesh=mesh, in_specs=in_specs, out_specs=out_specs, check_vma=False)(
            qkv_grad, master, moment_one, moment_two, average, step
        )

    return run
```

```python
import functools
import math

import jax
import jax.numpy as jnp
from jax import lax
from jax.experimental import pallas as pl
from jax.experimental.pallas import tpu as pltpu
from jax.sharding import PartitionSpec as P

MESH = pl.DeviceIdType.MESH
DEPTH = 6
LAG = 2
KEPT = 1
WIDE = 4


def step_kernel(
    sizes, limit, step, x, master, one, two, average,
    w_low, w_high, out_master, out_one, out_two, out_average,
    held, inbox, gbox, half, extra, square, zbox, pbox,
    x_sem, state_sem, send, wide_send, recv, extra_send, extra_recv, sum_send, sum_recv, z_send, z_recv, p_sem,
    y_send, y_recv,
):
    shards, groups, sections = sizes
    s, t, c = lax.axis_index("shard"), lax.axis_index("tensor"), lax.axis_index("section")
    last = shards - 1
    near = shards // 2
    _, _, rows, cols = x.shape
    tile = inbox.shape[2]
    tiles = rows // tile
    share = groups * tiles
    count = near * share
    plane = groups * sections
    depth = max(DEPTH, groups)
    wide = widest(tiles)
    blocks = share // wide
    at_end = jnp.logical_or(s == 0, s == last)
    at_near = jnp.logical_or(s == 1, s == last - 1)
    kept = split(shards, tiles)
    holders = [0, last] + ([1, last - 1] if kept else [])

    def load(q, g):
        return pltpu.make_async_copy(x.at[q, g], held.at[q, g], x_sem.at[q, g])

    def fetch(n):
        for g in range(groups):
            @pl.when(s > 0)
            def _():
                load(last - n, g).start()

            @pl.when(s < last)
            def _():
                load(n, g).start()

    states = [
        pltpu.make_async_copy(src, dst, state_sem.at[n])
        for n, (src, dst) in enumerate(
            ((master, out_master), (one, out_one), (two, out_two), (average, out_average))
        )
    ]

    barrier = pltpu.get_barrier_semaphore()

    def peer(off):
        at = lax.rem(t * sections + c + off, plane)
        return {"tensor": lax.div(at, sections), "section": lax.rem(at, sections)}

    @pl.loop(1, plane)
    def _(off):
        pl.semaphore_signal(barrier, inc=1, device_id=peer(off), device_id_type=MESH)

    @pl.loop(groups, shards * groups)
    def _(off):
        pl.semaphore_signal(
            barrier,
            inc=1,
            device_id={
                "shard": lax.rem(s + lax.div(off, groups), shards),
                "tensor": lax.rem(t + lax.rem(off, groups), groups),
            },
            device_id_type=MESH,
        )

    fetch(0)
    square[...] = jnp.zeros_like(square)
    zbox[...] = jnp.zeros_like(zbox)
    pl.semaphore_wait(barrier, plane - 1 + (shards - 1) * groups)

    def place(way, i):
        n, rest = lax.div(i, share), lax.rem(i, share)
        j, g = lax.div(rest, groups), lax.rem(rest, groups)
        return (last - n if way == 0 else n), g, j

    def short_of(way, q, j):
        return jnp.logical_and(q == (last - 1 if way == 0 else 1), j >= tiles - kept)

    def part(j):
        return pl.ds(pl.multiple_of(j * tile, tile), tile)

    def hop(way, i, src):
        return pltpu.make_async_remote_copy(
            src_ref=src,
            dst_ref=inbox.at[way, i],
            send_sem=send.at[way, lax.rem(i, depth)],
            recv_sem=recv.at[way, i],
            device_id={"shard": jnp.minimum(s + 1, last) if way == 0 else jnp.maximum(s - 1, 0)},
            device_id_type=MESH,
        )

    def spare(g, j, q=0):
        e = (j - (tiles - kept)) * groups + g
        return pltpu.make_async_remote_copy(
            src_ref=x.at[q, g, part(j)],
            dst_ref=extra.at[e],
            send_sem=extra_send.at[e],
            recv_sem=extra_recv.at[e],
            device_id={"shard": jnp.where(s == 0, 1, last - 1)},
            device_id_type=MESH,
        )

    def spares(use):
        for q, where in ((1, 0), (last - 1, last)):
            @pl.when(s == where)
            def _():
                for j in range(tiles - kept, tiles):
                    for g in range(groups):
                        use(spare(g, j, q))

    def hand(way, i):
        q, g, j = place(way, i)
        return pltpu.make_async_remote_copy(
            src_ref=inbox.at[way, i],
            dst_ref=gbox.at[t, part(j)],
            send_sem=sum_send.at[jnp.where(q == s, 0, 1)],
            recv_sem=sum_recv.at[t, j],
            device_id={"shard": q, "tensor": g},
            device_id_type=MESH,
        )

    def summed(g, j):
        return pltpu.make_async_remote_copy(
            src_ref=gbox.at[g, part(j)],
            dst_ref=gbox.at[g, part(j)],
            send_sem=sum_send.at[0],
            recv_sem=sum_recv.at[g, j],
            device_id={"tensor": g},
            device_id_type=MESH,
        )

    @pl.loop(0, count + LAG * last)
    def _(now):
        @pl.when(now == 1)
        def _():
            for n in range(1, near):
                fetch(n)

        @pl.when(now == LAG * last)
        def _():
            for copy in states:
                copy.start()

        for way in (0, 1):
            lag = s if way == 0 else last - s
            i = now - LAG * lag
            q, g, j = place(way, i)
            cut = short_of(way, q, j)
            stop = jnp.where(cut, last - 1, last)

            def finish(acc):
                short = acc.astype(jnp.bfloat16)
                square[...] += jnp.sum((acc * acc).reshape(tile // 8, 8, cols), axis=0)
                mine = jnp.logical_and(q == s, g == t)

                @pl.when(mine)
                def _():
                    gbox[t, part(j)] = short

                @pl.when(jnp.logical_not(mine))
                def _():
                    inbox[way, i] = short

                @pl.when(jnp.logical_and(q == s, g != t))
                def _():
                    hand(way, i).start()

            @pl.when(jnp.logical_and(jnp.logical_and(i >= 0, i < count), lag <= stop))
            def _():
                before_q, _, before_j = place(way, i - depth)
                before_cut = short_of(way, before_q, before_j)
                before_stop = jnp.where(before_cut, last - 1, last)

                @pl.when(jnp.logical_and(lag < before_stop, i >= depth))
                def _():
                    hop(way, i - depth, inbox.at[way, i - depth]).wait_send()

                @pl.when(lag == 0)
                def _():
                    hop(way, i, x.at[q, g, part(j)]).start()

                @pl.when(lag > 0)
                def _():
                    @pl.when(j == 0)
                    def _():
                        load(q, g).wait()

                    hop(way, i, inbox.at[way, i]).wait_recv()
                    acc = inbox[way, i].astype(jnp.float32) + held[q, g, part(j)].astype(jnp.float32)

                    @pl.when(lag < stop)
                    def _():
                        inbox[way, i] = acc.astype(jnp.bfloat16)
                        hop(way, i, inbox.at[way, i]).start()

                    @pl.when(jnp.logical_and(lag == stop, jnp.logical_not(cut)))
                    def _():
                        finish(acc)

                    if kept:
                        @pl.when(jnp.logical_and(lag == stop, cut))
                        def _():
                            spare(g, j).wait_recv()
                            e = (j - (tiles - kept)) * groups + g
                            finish(acc + extra[e].astype(jnp.float32))

        if kept:
            @pl.when(now == count - 1)
            def _():
                spares(lambda copy: copy.start())

    def spread(off):
        return pltpu.make_async_remote_copy(
            src_ref=zbox.at[s],
            dst_ref=zbox.at[s],
            send_sem=z_send.at[0],
            recv_sem=z_recv.at[s],
            device_id={"shard": lax.rem(s + off, shards)},
            device_id_type=MESH,
        )

    def level(off):
        return pltpu.make_async_remote_copy(
            src_ref=pbox.at[0],
            dst_ref=pbox.at[off],
            send_sem=p_sem.at[0],
            recv_sem=p_sem.at[1],
            device_id=peer(off),
            device_id_type=MESH,
        )

    def settled(ref, sem):
        return pltpu.make_async_copy(ref, ref, sem)

    others = pbox.at[pl.ds(1, plane - 1)]

    def came(slot):
        return pltpu.make_async_copy(zbox.at[slot], zbox.at[slot], z_recv.at[slot])

    holding = jnp.logical_or(at_end, at_near) if kept else at_end

    @pl.when(holding)
    def _():
        narrow = square[:, :128]
        for n in range(1, cols // 128):
            narrow = narrow + square[:, n * 128 : (n + 1) * 128]
        zbox[s] = narrow

        @pl.loop(1, shards)
        def _(off):
            spread(off).start()

    for way, where in ((0, last), (1, 0)):
        @pl.when(s == where)
        def _():
            @pl.loop(share, count)
            def _(i):
                q, _, j = place(way, i)

                @pl.when(jnp.logical_not(short_of(way, q, j)))
                def _():
                    hand(way, i).start()

    for holder in holders:
        @pl.when(s != holder)
        def _():
            came(holder).wait()

    total = zbox[holders[0]]
    for holder in holders[1:]:
        total = total + zbox[holder]
    pbox[0] = total

    @pl.loop(1, plane)
    def _(off):
        level(off).start()

    for way, here in ((0, s < last), (1, s > 0)):
        @pl.when(here)
        def _():
            @pl.loop(max(count - depth, 0), count)
            def _(i):
                q, _, j = place(way, i)
                lag = s if way == 0 else last - s

                @pl.when(lag < jnp.where(short_of(way, q, j), last - 1, last))
                def _():
                    hop(way, i, inbox.at[way, i]).wait_send()

    for copy in states:
        copy.wait()
    times = jnp.full((8, 128), step[0].astype(jnp.float32))
    first_fix = jnp.max(1.0 / (1.0 - jnp.exp(times * math.log(0.9))))
    second_fix = jnp.max(1.0 / (1.0 - jnp.exp(times * math.log(0.95))))

    settled(others, p_sem.at[1]).wait()

    whole = pbox[0]
    for n in range(1, plane):
        whole = whole + pbox[n]
    norm = jnp.sqrt(jnp.full((8, 128), jnp.sum(whole)))
    clip = jnp.max(jnp.minimum(1.0, limit / (norm + 1e-06)))

    def within(p, use):
        @pl.when(p < near)
        def _():
            use(w_low, p)

        @pl.when(p >= near)
        def _():
            use(w_high, p - near)

    def cross(k, j, w=w_low, row=0):
        return pltpu.make_async_remote_copy(
            src_ref=half.at[k - 1, part(j)],
            dst_ref=w.at[row, t, part(j)],
            send_sem=y_send.at[0],
            recv_sem=y_recv.at[k - 1, j],
            device_id={"tensor": lax.rem(t + k, groups)},
            device_id_type=MESH,
        )

    def crossed(k, j):
        g = lax.rem(t + k, groups)
        return pltpu.make_async_remote_copy(
            src_ref=w_low.at[0, g, part(j)],
            dst_ref=w_low.at[0, g, part(j)],
            send_sem=y_send.at[0],
            recv_sem=y_recv.at[groups - k - 1, j],
            device_id={"tensor": g},
            device_id_type=MESH,
        )

    def onward(way):
        return jnp.minimum(s + 1, last) if way == 0 else jnp.maximum(s - 1, 0)

    def emit(way, n, w=w_low, row=0):
        j, k = lax.div(n, groups), lax.rem(n, groups)
        block = w.at[row, lax.rem(t + k, groups), part(j)]
        return pltpu.make_async_remote_copy(
            src_ref=block,
            dst_ref=block,
            send_sem=send.at[way, lax.rem(n, depth)],
            recv_sem=recv.at[way, n],
            device_id={"shard": onward(way)},
            device_id_type=MESH,
        )

    def forward(way, n, w=w_low, row=0):
        b = lax.rem(n, blocks)
        j, k = lax.div(b, groups), lax.rem(b, groups)
        block = w.at[row, lax.rem(t + k, groups), pl.ds(pl.multiple_of(j * wide * tile, wide * tile), wide * tile)]
        return pltpu.make_async_remote_copy(
            src_ref=block,
            dst_ref=block,
            send_sem=wide_send.at[way, lax.rem(n, 2)],
            recv_sem=recv.at[way, share + n],
            device_id={"shard": onward(way)},
            device_id_type=MESH,
        )

    def both(n):
        for way in (0, 1):
            @pl.when(s < last if way == 0 else s > 0)
            def _():
                @pl.when(n >= depth)
                def _():
                    emit(way, n - depth).wait_send()

                within(s, lambda w, row: emit(way, n, w, row).start())

    def relay(way, n):
        reach = s if way == 0 else last - s

        @pl.when(n < reach * blocks)
        def _():
            @pl.when(n < blocks)
            def _():
                j, k = lax.div(n, groups), lax.rem(n, groups)
                for e in range(wide):
                    emit(way, (j * wide + e) * groups + k).wait_recv()

            @pl.when(n >= blocks)
            def _():
                forward(way, n - blocks).wait_recv()

            @pl.when(s < last if way == 0 else s > 0)
            def _():
                @pl.when(n >= 2)
                def _():
                    forward(way, n - 2).wait_send()

                away = lax.div(n, blocks) + 1
                p = s - away if way == 0 else s + away
                within(p, lambda w, row: forward(way, n, w, row).start())

    @pl.loop(0, share + groups)
    def _(now):
        j, k = lax.div(now, groups), lax.rem(now, groups)
        g = lax.rem(t + k, groups)

        @pl.when(now < share)
        def _():
            there = pl.ds(pl.multiple_of(g * cols, 128), cols)

            local = jnp.logical_or(at_end, jnp.logical_and(at_near, j >= tiles - kept)) if kept else at_end

            @pl.when(jnp.logical_not(jnp.logical_and(local, k == 0)))
            def _():
                summed(g, j).wait_recv()

            clipped = clip * gbox[g, part(j)].astype(jnp.float32)
            new_one = 0.9 * out_one[part(j), there] + 0.1 * clipped
            new_two = 0.95 * out_two[part(j), there] + 0.05 * clipped * clipped
            update = new_one * first_fix / (jnp.sqrt(new_two * second_fix) + 1e-08)
            new_master = out_master[part(j), there] * (1.0 - 0.1 * 0.1) - 0.1 * update
            out_one[part(j), there] = new_one
            out_two[part(j), there] = new_two
            out_master[part(j), there] = new_master
            short = new_master.astype(jnp.bfloat16)

            @pl.when(k == 0)
            def _():
                def keep(w, row):
                    w[row, t, part(j)] = short

                within(s, keep)
                both(now)

            @pl.when(k > 0)
            def _():
                half[k - 1, part(j)] = short
                within(s, lambda w, row: cross(k, j, w, row).start())

        @pl.when(jnp.logical_and(k > 0, now >= groups))
        def _():
            crossed(k, j - 1).wait_recv()
            both(now - groups)

    @pl.loop(0, last * blocks)
    def _(n):
        @pl.when(s < near)
        def _():
            relay(1, n)
            relay(0, n)

        @pl.when(s >= near)
        def _():
            relay(0, n)
            relay(1, n)

        @pl.when(n < blocks)
        def _():
            @pl.loop(0, wide)
            def _(e):
                m = n * wide + e
                j, g = lax.div(m, groups), lax.rem(m, groups)

                def mix(w, row):
                    fresh = w[row, g, part(j)].astype(jnp.float32)
                    out_average[g, part(j)] = 0.99 * out_average[g, part(j)] + 0.01 * fresh

                within(s, mix)

    for way in (0, 1):
        reach = s if way == 0 else last - s

        @pl.when(s < last if way == 0 else s > 0)
        def _():
            @pl.loop(max(share - depth, 0), share)
            def _(n):
                emit(way, n).wait_send()

            for n in (2, 1):
                @pl.when(reach * blocks >= n)
                def _():
                    forward(way, reach * blocks - n).wait_send()

    if groups > 1:
        settled(half, y_send.at[0]).wait()

        @pl.when(at_end)
        def _():
            settled(inbox.at[0, pl.ds(0, tiles * (groups - 1))], sum_send.at[0]).wait()

    late = count - share - kept * groups
    if late:
        @pl.when(at_end)
        def _():
            settled(inbox.at[0, pl.ds(0, late)], sum_send.at[1]).wait()

    if kept:
        spares(lambda copy: copy.wait_send())

        if groups > 1:
            @pl.when(at_near)
            def _():
                settled(inbox.at[0, pl.ds(0, kept * (groups - 1))], sum_send.at[0]).wait()

    @pl.when(holding)
    def _():
        settled(zbox.at[pl.ds(0, last)], z_send.at[0]).wait()

    settled(others, p_sem.at[0]).wait()


def widest(tiles):
    return next(n for n in (WIDE, 2, 1) if tiles % n == 0)


def split(shards, tiles):
    return KEPT if shards >= 4 and tiles > KEPT else 0


def adam_step(sizes, limit, step, x, master, one, two, average):
    shards, groups, sections = sizes
    _, _, rows, cols = x.shape
    tile = min(rows, 16)
    tiles = rows // tile
    share = groups * tiles
    count = shards // 2 * share
    plane = groups * sections
    dma = pltpu.SemaphoreType.DMA
    anywhere = pl.BlockSpec(memory_space=pl.ANY)
    near = pl.BlockSpec(memory_space=pltpu.VMEM)
    state = jax.ShapeDtypeStruct(master.shape, jnp.float32)
    weights = jax.ShapeDtypeStruct((shards // 2,) + x.shape[1:], jnp.bfloat16)
    return pl.pallas_call(
        functools.partial(step_kernel, sizes, limit),
        out_shape=[
            weights,
            weights,
            state,
            state,
            state,
            jax.ShapeDtypeStruct(average.shape, jnp.float32),
        ],
        in_specs=[pl.BlockSpec(memory_space=pltpu.SMEM)] + [anywhere] * 5,
        out_specs=[near] * 6,
        scratch_shapes=[
            pltpu.VMEM(x.shape, jnp.bfloat16),
            pltpu.VMEM((2, count, tile, cols), jnp.bfloat16),
            pltpu.VMEM((groups, rows, cols), jnp.bfloat16),
            pltpu.VMEM((max(groups - 1, 1), rows, cols), jnp.bfloat16),
            pltpu.VMEM((max(split(shards, tiles), 1) * groups, tile, cols), jnp.bfloat16),
            pltpu.VMEM((8, cols), jnp.float32),
            pltpu.VMEM((shards, 8, 128), jnp.float32),
            pltpu.VMEM((plane, 8, 128), jnp.float32),
            dma((shards, groups)),
            dma((4,)),
            dma((2, max(DEPTH, groups))),
            dma((2, 2)),
            dma((2, max(count, share + (shards - 2) * (share // widest(tiles))))),
            dma((max(split(shards, tiles), 1) * groups,)),
            dma((max(split(shards, tiles), 1) * groups,)),
            dma((2,)),
            dma((groups, tiles)),
            dma((1,)),
            dma((shards,)),
            dma((2,)),
            dma((1,)),
            dma((max(groups - 1, 1), tiles)),
        ],
        compiler_params=pltpu.CompilerParams(
            collective_id=0, has_side_effects=True, vmem_limit_bytes=34 * 2**20
        ),
    )(step, x, master, one, two, average)


def store_kernel(low, high, master, one, two, average, w, *rest):
    outs, sem = rest[:-1], rest[-1]
    half = low.shape[0]
    pairs = [(low, w.at[pl.ds(0, half)]), (high, w.at[pl.ds(half, half)])]
    pairs += zip((master, one, two, average), outs)
    copies = [pltpu.make_async_copy(src, dst, sem.at[n]) for n, (src, dst) in enumerate(pairs)]
    for copy in copies:
        copy.start()
    for copy in copies:
        copy.wait()


def store(low, high, *arrays):
    shape = (2 * low.shape[0],) + low.shape[1:]
    return pl.pallas_call(
        store_kernel,
        out_shape=[jax.ShapeDtypeStruct(shape, low.dtype)]
        + [jax.ShapeDtypeStruct(a.shape, a.dtype) for a in arrays],
        in_specs=[pl.BlockSpec(memory_space=pltpu.VMEM)] * (len(arrays) + 2),
        out_specs=[pl.BlockSpec(memory_space=pl.ANY)] * (len(arrays) + 1),
        scratch_shapes=[pltpu.SemaphoreType.DMA((len(arrays) + 2,))],
        compiler_params=pltpu.CompilerParams(vmem_limit_bytes=34 * 2**20),
    )(low, high, *arrays)


def body(sizes, limit, qkv_grad, master, moment_one, moment_two, average, step):
    shards, groups, _ = sizes
    rows = qkv_grad.shape[1] // (shards * groups)
    cols = qkv_grad.shape[2]
    parts = adam_step(
        sizes,
        limit,
        step.reshape(1),
        qkv_grad.reshape(shards, groups, rows, cols),
        master,
        moment_one,
        moment_two,
        average.reshape(groups, rows, cols),
    )
    weights, new_master, new_one, new_two, new_average = store(*parts)
    return (
        weights.reshape(shards * groups * rows, cols),
        new_master,
        new_one,
        new_two,
        new_average.reshape(average.shape),
    )


def solution(mesh):
    state = P(("section", "shard", "tensor"), None)
    in_specs = (
        P("shard", "section", "tensor"),
        state,
        state,
        state,
        P(("section", "shard"), "tensor"),
        P(),
    )
    out_specs = (
        P("section", "tensor"),
        state,
        state,
        state,
        P(("section", "shard"), "tensor"),
    )
    sizes = tuple(mesh.shape[name] for name in ("shard", "tensor", "section"))

    def run(qkv_grad, master, moment_one, moment_two, average, step):
        limit = math.sqrt(master.shape[0] * master.shape[1])
        fn = functools.partial(body, sizes, limit)
        return jax.shard_map(fn, mesh=mesh, in_specs=in_specs, out_specs=out_specs, check_vma=False)(
            qkv_grad, master, moment_one, moment_two, average, step
        )

    return run
```

```python
import functools
import math

import jax
import jax.numpy as jnp
from jax import lax
from jax.experimental import pallas as pl
from jax.experimental.pallas import tpu as pltpu
from jax.sharding import PartitionSpec as P

MESH = pl.DeviceIdType.MESH
DEPTH = 6
LAG = 2
KEPT = 1
WIDE = 4


def step_kernel(
    sizes, limit, step, x, master, one, two, average,
    w_low, w_high, out_master, out_one, out_two, out_average,
    held, inbox, gbox, half, extra, early, gtile, wtile, other, square, zbox, pbox,
    x_sem, state_sem, send, wide_send, recv, extra_send, extra_recv, early_load, early_send, early_recv, sum_send, sum_recv, z_send, z_recv, p_sem,
    y_send, y_recv,
):
    shards, groups, sections = sizes
    s, t, c = lax.axis_index("shard"), lax.axis_index("tensor"), lax.axis_index("section")
    last = shards - 1
    near = shards // 2
    _, _, rows, cols = x.shape
    tile = inbox.shape[2]
    tiles = rows // tile
    share = groups * tiles
    count = near * share
    plane = groups * sections
    depth = max(DEPTH, groups)
    wide = widest(tiles)
    blocks = share // wide
    at_end = jnp.logical_or(s == 0, s == last)
    at_near = jnp.logical_or(s == 1, s == last - 1)
    kept = split(shards, tiles)
    holders = [0, last] + ([1, last - 1] if kept else [])
    told = tiles - kept - 1
    seat = t * sections + c

    def load(q, g):
        return pltpu.make_async_copy(x.at[q, g], held.at[q, g], x_sem.at[q, g])

    def fetch(n):
        for g in range(groups):
            @pl.when(s > 0)
            def _():
                load(last - n, g).start()

            @pl.when(s < last)
            def _():
                load(n, g).start()

    states = [
        pltpu.make_async_copy(src, dst, state_sem.at[n])
        for n, (src, dst) in enumerate(
            ((master, out_master), (one, out_one), (two, out_two), (average, out_average))
        )
    ]

    barrier = pltpu.get_barrier_semaphore()

    def peer(off):
        at = lax.rem(seat + off, plane)
        return {"tensor": lax.div(at, sections), "section": lax.rem(at, sections)}

    @pl.loop(1, plane)
    def _(off):
        pl.semaphore_signal(barrier, inc=1, device_id=peer(off), device_id_type=MESH)

    @pl.loop(groups, shards * groups)
    def _(off):
        pl.semaphore_signal(
            barrier,
            inc=1,
            device_id={
                "shard": lax.rem(s + lax.div(off, groups), shards),
                "tensor": lax.rem(t + lax.rem(off, groups), groups),
            },
            device_id_type=MESH,
        )

    def part(j):
        return pl.ds(pl.multiple_of(j * tile, tile), tile)

    if kept:
        firsts = [
            pltpu.make_async_copy(src.at[part(told)], dst.at[part(told)], early_load.at[n])
            for n, (src, dst) in enumerate(((master, out_master), (one, out_one), (two, out_two)))
        ]

        @pl.when(at_near)
        def _():
            for copy in firsts:
                copy.start()

    fetch(0)
    square[...] = jnp.zeros_like(square)
    zbox[...] = jnp.zeros_like(zbox)

    def tell(k):
        return pltpu.make_async_remote_copy(
            src_ref=early.at[k],
            dst_ref=early.at[t],
            send_sem=early_send.at[k],
            recv_sem=early_recv.at[t],
            device_id={"shard": jnp.where(s == 1, 0, last), "tensor": lax.rem(t + k, groups)},
            device_id_type=MESH,
        )

    if kept:
        @pl.when(at_near)
        def _():
            for n, (copy, ref) in enumerate(zip(firsts, (out_master, out_one, out_two))):
                copy.wait()

                @pl.loop(0, groups)
                def _(k):
                    there = pl.ds(pl.multiple_of(lax.rem(t + k, groups) * cols, 128), cols)
                    early[k, n] = ref[part(told), there].astype(jnp.bfloat16)

    pl.semaphore_wait(barrier, plane - 1 + (shards - 1) * groups)

    if kept:
        @pl.when(at_near)
        def _():
            tell(0).start()


    def place(way, i):
        n, rest = lax.div(i, share), lax.rem(i, share)
        j, g = lax.div(rest, groups), lax.rem(rest, groups)
        return (last - n if way == 0 else n), g, j

    def short_of(way, q, j):
        return jnp.logical_and(q == (last - 1 if way == 0 else 1), j >= tiles - kept)

    def hop(way, i, src):
        return pltpu.make_async_remote_copy(
            src_ref=src,
            dst_ref=inbox.at[way, i],
            send_sem=send.at[way, lax.rem(i, depth)],
            recv_sem=recv.at[way, i],
            device_id={"shard": jnp.minimum(s + 1, last) if way == 0 else jnp.maximum(s - 1, 0)},
            device_id_type=MESH,
        )

    def spare(g, j, q=0):
        e = (j - (tiles - kept)) * groups + g
        return pltpu.make_async_remote_copy(
            src_ref=x.at[q, g, part(j)],
            dst_ref=extra.at[e],
            send_sem=extra_send.at[e],
            recv_sem=extra_recv.at[e],
            device_id={"shard": jnp.where(s == 0, 1, last - 1)},
            device_id_type=MESH,
        )

    def spares(use):
        for q, where in ((1, 0), (last - 1, last)):
            @pl.when(s == where)
            def _():
                for j in range(tiles - kept, tiles):
                    for g in range(groups):
                        use(spare(g, j, q))

    def hand(way, i):
        q, g, j = place(way, i)
        return pltpu.make_async_remote_copy(
            src_ref=inbox.at[way, i],
            dst_ref=gbox.at[t, part(j)],
            send_sem=sum_send.at[jnp.where(q == s, 0, 1)],
            recv_sem=sum_recv.at[t, j],
            device_id={"shard": q, "tensor": g},
            device_id_type=MESH,
        )

    def summed(g, j):
        return pltpu.make_async_remote_copy(
            src_ref=gbox.at[g, part(j)],
            dst_ref=gbox.at[g, part(j)],
            send_sem=sum_send.at[0],
            recv_sem=sum_recv.at[g, j],
            device_id={"tensor": g},
            device_id_type=MESH,
        )

    @pl.loop(0, count + LAG * last)
    def _(now):
        @pl.when(now == 1)
        def _():
            for n in range(1, near):
                fetch(n)

        @pl.when(now == LAG * last)
        def _():
            for copy in states:
                copy.start()

        for way in (0, 1):
            lag = s if way == 0 else last - s
            i = now - LAG * lag
            q, g, j = place(way, i)
            cut = short_of(way, q, j)
            stop = jnp.where(cut, last - 1, last)

            def finish(acc):
                short = acc.astype(jnp.bfloat16)
                square[...] += jnp.sum((acc * acc).reshape(tile // 8, 8, cols), axis=0)
                mine = jnp.logical_and(q == s, g == t)

                @pl.when(mine)
                def _():
                    gbox[t, part(j)] = short

                @pl.when(jnp.logical_not(mine))
                def _():
                    inbox[way, i] = short

                @pl.when(jnp.logical_and(q == s, g != t))
                def _():
                    hand(way, i).start()

            @pl.when(jnp.logical_and(jnp.logical_and(i >= 0, i < count), lag <= stop))
            def _():
                before_q, _, before_j = place(way, i - depth)
                before_cut = short_of(way, before_q, before_j)
                before_stop = jnp.where(before_cut, last - 1, last)

                @pl.when(jnp.logical_and(lag < before_stop, i >= depth))
                def _():
                    hop(way, i - depth, inbox.at[way, i - depth]).wait_send()

                @pl.when(lag == 0)
                def _():
                    hop(way, i, x.at[q, g, part(j)]).start()

                @pl.when(lag > 0)
                def _():
                    @pl.when(j == 0)
                    def _():
                        load(q, g).wait()

                    hop(way, i, inbox.at[way, i]).wait_recv()
                    acc = inbox[way, i].astype(jnp.float32) + held[q, g, part(j)].astype(jnp.float32)

                    @pl.when(lag < stop)
                    def _():
                        inbox[way, i] = acc.astype(jnp.bfloat16)
                        hop(way, i, inbox.at[way, i]).start()

                    @pl.when(jnp.logical_and(lag == stop, jnp.logical_not(cut)))
                    def _():
                        finish(acc)

                    if kept:
                        @pl.when(jnp.logical_and(lag == stop, cut))
                        def _():
                            spare(g, j).wait_recv()
                            e = (j - (tiles - kept)) * groups + g
                            finish(acc + extra[e].astype(jnp.float32))

        if kept:
            @pl.when(now == count - 1)
            def _():
                spares(lambda copy: copy.start())

    def spread(off):
        return pltpu.make_async_remote_copy(
            src_ref=zbox.at[s],
            dst_ref=zbox.at[s],
            send_sem=z_send.at[0],
            recv_sem=z_recv.at[s],
            device_id={"shard": lax.rem(s + off, shards)},
            device_id_type=MESH,
        )

    def level(off):
        return pltpu.make_async_remote_copy(
            src_ref=pbox.at[seat],
            dst_ref=pbox.at[seat],
            send_sem=p_sem.at[0],
            recv_sem=p_sem.at[1],
            device_id=peer(off),
            device_id_type=MESH,
        )

    def settled(ref, sem):
        return pltpu.make_async_copy(ref, ref, sem)

    others = pbox.at[pl.ds(0, plane - 1)]

    def came(slot):
        return pltpu.make_async_copy(zbox.at[slot], zbox.at[slot], z_recv.at[slot])

    holding = jnp.logical_or(at_end, at_near) if kept else at_end

    @pl.when(holding)
    def _():
        narrow = square[:, :128]
        for n in range(1, cols // 128):
            narrow = narrow + square[:, n * 128 : (n + 1) * 128]
        zbox[s] = narrow

        @pl.loop(1, shards)
        def _(off):
            spread(off).start()

    if kept:
        @pl.when(at_near)
        def _():
            @pl.loop(1, groups)
            def _(k):
                tell(k).start()

    for way, where in ((0, last), (1, 0)):
        @pl.when(s == where)
        def _():
            @pl.loop(share, count)
            def _(i):
                q, _, j = place(way, i)

                @pl.when(jnp.logical_not(short_of(way, q, j)))
                def _():
                    hand(way, i).start()

    for holder in holders:
        @pl.when(s != holder)
        def _():
            came(holder).wait()

    total = zbox[holders[0]]
    for holder in holders[1:]:
        total = total + zbox[holder]
    pbox[seat] = total

    @pl.loop(1, plane)
    def _(off):
        level(off).start()

    for way, here in ((0, s < last), (1, s > 0)):
        @pl.when(here)
        def _():
            @pl.loop(max(count - depth, 0), count)
            def _(i):
                q, _, j = place(way, i)
                lag = s if way == 0 else last - s

                @pl.when(lag < jnp.where(short_of(way, q, j), last - 1, last))
                def _():
                    hop(way, i, inbox.at[way, i]).wait_send()

    for copy in states:
        copy.wait()
    times = jnp.full((8, 128), step[0].astype(jnp.float32))
    first_fix = jnp.max(1.0 / (1.0 - jnp.exp(times * math.log(0.9))))
    second_fix = jnp.max(1.0 / (1.0 - jnp.exp(times * math.log(0.95))))

    settled(others, p_sem.at[1]).wait()

    whole = pbox[0]
    for n in range(1, plane):
        whole = whole + pbox[n]
    norm = jnp.sqrt(jnp.full((8, 128), jnp.sum(whole)))
    clip = jnp.max(jnp.minimum(1.0, limit / (norm + 1e-06)))

    def within(p, use):
        @pl.when(p < near)
        def _():
            use(w_low, p)

        @pl.when(p >= near)
        def _():
            use(w_high, p - near)

    def cross(k, j, w=w_low, row=0):
        return pltpu.make_async_remote_copy(
            src_ref=half.at[k - 1, part(j)],
            dst_ref=w.at[row, t, part(j)],
            send_sem=y_send.at[0],
            recv_sem=y_recv.at[k - 1, j],
            device_id={"tensor": lax.rem(t + k, groups)},
            device_id_type=MESH,
        )

    def crossed(k, j):
        g = lax.rem(t + k, groups)
        return pltpu.make_async_remote_copy(
            src_ref=w_low.at[0, g, part(j)],
            dst_ref=w_low.at[0, g, part(j)],
            send_sem=y_send.at[0],
            recv_sem=y_recv.at[groups - k - 1, j],
            device_id={"tensor": g},
            device_id_type=MESH,
        )

    def onward(way):
        return jnp.minimum(s + 1, last) if way == 0 else jnp.maximum(s - 1, 0)

    def emit(way, n, w=w_low, row=0):
        j, k = lax.div(n, groups), lax.rem(n, groups)
        block = w.at[row, lax.rem(t + k, groups), part(j)]
        return pltpu.make_async_remote_copy(
            src_ref=block,
            dst_ref=block,
            send_sem=send.at[way, lax.rem(n, depth)],
            recv_sem=recv.at[way, n],
            device_id={"shard": onward(way)},
            device_id_type=MESH,
        )

    def forward(way, n, w=w_low, row=0):
        b = lax.rem(n, blocks)
        j, k = lax.div(b, groups), lax.rem(b, groups)
        block = w.at[row, lax.rem(t + k, groups), pl.ds(pl.multiple_of(j * wide * tile, wide * tile), wide * tile)]
        return pltpu.make_async_remote_copy(
            src_ref=block,
            dst_ref=block,
            send_sem=wide_send.at[way, lax.rem(n, 2)],
            recv_sem=recv.at[way, share + n],
            device_id={"shard": onward(way)},
            device_id_type=MESH,
        )

    def sent(way, n):
        ends_next = s == (last - 1 if way == 0 else 1)
        return jnp.logical_not(
            jnp.logical_and(jnp.logical_and(ends_next, lax.div(n, groups) == told), kept > 0)
        )

    def both(n):
        for way in (0, 1):
            @pl.when(s < last if way == 0 else s > 0)
            def _():
                @pl.when(jnp.logical_and(n >= depth, sent(way, n - depth)))
                def _():
                    emit(way, n - depth).wait_send()

                @pl.when(sent(way, n))
                def _():
                    within(s, lambda w, row: emit(way, n, w, row).start())

    def relay(way, n):
        reach = s if way == 0 else last - s

        @pl.when(n < reach * blocks)
        def _():
            @pl.when(n < blocks)
            def _():
                j, k = lax.div(n, groups), lax.rem(n, groups)
                for e in range(wide):
                    row = j * wide + e

                    @pl.when(jnp.logical_not(jnp.logical_and(jnp.logical_and(at_end, row == told), kept > 0)))
                    def _():
                        emit(way, row * groups + k).wait_recv()

            @pl.when(n >= blocks)
            def _():
                forward(way, n - blocks).wait_recv()

            @pl.when(s < last if way == 0 else s > 0)
            def _():
                @pl.when(n >= 2)
                def _():
                    forward(way, n - 2).wait_send()

                away = lax.div(n, blocks) + 1
                p = s - away if way == 0 else s + away
                within(p, lambda w, row: forward(way, n, w, row).start())

    def adam(grad, old, first, second):
        clipped = clip * grad.astype(jnp.float32)
        new_one = 0.9 * first + 0.1 * clipped
        new_two = 0.95 * second + 0.05 * clipped * clipped
        update = new_one * first_fix / (jnp.sqrt(new_two * second_fix) + 1e-08)
        return old * (1.0 - 0.1 * 0.1) - 0.1 * update, new_one, new_two

    @pl.loop(0, share + groups)
    def _(now):
        j, k = lax.div(now, groups), lax.rem(now, groups)
        g = lax.rem(t + k, groups)

        @pl.when(now < share)
        def _():
            there = pl.ds(pl.multiple_of(g * cols, 128), cols)

            local = jnp.logical_or(at_end, jnp.logical_and(at_near, j >= tiles - kept)) if kept else at_end

            @pl.when(jnp.logical_not(jnp.logical_and(local, k == 0)))
            def _():
                summed(g, j).wait_recv()

            new_master, new_one, new_two = adam(
                gbox[g, part(j)], out_master[part(j), there], out_one[part(j), there], out_two[part(j), there]
            )
            out_one[part(j), there] = new_one
            out_two[part(j), there] = new_two
            out_master[part(j), there] = new_master
            wtile[...] = new_master.astype(jnp.bfloat16)

            if kept:
                @pl.when(jnp.logical_and(jnp.logical_or(at_end, at_near), j == told))
                def _():
                    @pl.when(at_near)
                    def _():
                        gtile[...] = gbox[g, part(j)]

                    @pl.when(at_end)
                    def _():
                        settled(early.at[k], early_recv.at[k]).wait()
                        gtile[...] = inbox[jnp.where(s == 0, 1, 0), share + told * groups + k]
                        other[...] = wtile[...]

                    rough = [early[k, n].astype(jnp.float32) for n in range(3)]
                    wtile[...] = adam(gtile[...], *rough)[0].astype(jnp.bfloat16)

                    @pl.when(at_end)
                    def _():
                        def keep(w, row):
                            w[row, k, part(j)] = wtile[...]

                        within(jnp.where(s == 0, 1, last - 1), keep)
                        wtile[...] = other[...]

            short = wtile[...]

            @pl.when(k == 0)
            def _():
                def keep(w, row):
                    w[row, t, part(j)] = short

                within(s, keep)
                both(now)

            @pl.when(k > 0)
            def _():
                half[k - 1, part(j)] = short
                within(s, lambda w, row: cross(k, j, w, row).start())

        @pl.when(jnp.logical_and(k > 0, now >= groups))
        def _():
            crossed(k, j - 1).wait_recv()
            both(now - groups)

    @pl.loop(0, last * blocks)
    def _(n):
        @pl.when(s < near)
        def _():
            relay(1, n)
            relay(0, n)

        @pl.when(s >= near)
        def _():
            relay(0, n)
            relay(1, n)

        @pl.when(n < blocks)
        def _():
            @pl.loop(0, wide)
            def _(e):
                m = n * wide + e
                j, g = lax.div(m, groups), lax.rem(m, groups)

                def mix(w, row):
                    fresh = w[row, g, part(j)].astype(jnp.float32)
                    out_average[g, part(j)] = 0.99 * out_average[g, part(j)] + 0.01 * fresh

                within(s, mix)

    for way in (0, 1):
        reach = s if way == 0 else last - s

        @pl.when(s < last if way == 0 else s > 0)
        def _():
            @pl.loop(max(share - depth, 0), share)
            def _(n):
                @pl.when(sent(way, n))
                def _():
                    emit(way, n).wait_send()

            for n in (2, 1):
                @pl.when(reach * blocks >= n)
                def _():
                    forward(way, reach * blocks - n).wait_send()

    if groups > 1:
        settled(half, y_send.at[0]).wait()

        @pl.when(at_end)
        def _():
            settled(inbox.at[0, pl.ds(0, tiles * (groups - 1))], sum_send.at[0]).wait()

    late = count - share - kept * groups
    if late:
        @pl.when(at_end)
        def _():
            settled(inbox.at[0, pl.ds(0, late)], sum_send.at[1]).wait()

    if kept:
        spares(lambda copy: copy.wait_send())

        @pl.when(at_near)
        def _():
            @pl.loop(0, groups)
            def _(k):
                tell(k).wait_send()

        if groups > 1:
            @pl.when(at_near)
            def _():
                settled(inbox.at[0, pl.ds(0, kept * (groups - 1))], sum_send.at[0]).wait()

    @pl.when(holding)
    def _():
        settled(zbox.at[pl.ds(0, last)], z_send.at[0]).wait()

    settled(others, p_sem.at[0]).wait()


def widest(tiles):
    return next(n for n in (WIDE, 2, 1) if tiles % n == 0)


def split(shards, tiles):
    return KEPT if shards >= 4 and tiles > KEPT else 0


def adam_step(sizes, limit, step, x, master, one, two, average):
    shards, groups, sections = sizes
    _, _, rows, cols = x.shape
    tile = min(rows, 16)
    tiles = rows // tile
    share = groups * tiles
    count = shards // 2 * share
    plane = groups * sections
    dma = pltpu.SemaphoreType.DMA
    anywhere = pl.BlockSpec(memory_space=pl.ANY)
    near = pl.BlockSpec(memory_space=pltpu.VMEM)
    state = jax.ShapeDtypeStruct(master.shape, jnp.float32)
    weights = jax.ShapeDtypeStruct((shards // 2,) + x.shape[1:], jnp.bfloat16)
    return pl.pallas_call(
        functools.partial(step_kernel, sizes, limit),
        out_shape=[
            weights,
            weights,
            state,
            state,
            state,
            jax.ShapeDtypeStruct(average.shape, jnp.float32),
        ],
        in_specs=[pl.BlockSpec(memory_space=pltpu.SMEM)] + [anywhere] * 5,
        out_specs=[near] * 6,
        scratch_shapes=[
            pltpu.VMEM(x.shape, jnp.bfloat16),
            pltpu.VMEM((2, count, tile, cols), jnp.bfloat16),
            pltpu.VMEM((groups, rows, cols), jnp.bfloat16),
            pltpu.VMEM((max(groups - 1, 1), rows, cols), jnp.bfloat16),
            pltpu.VMEM((max(split(shards, tiles), 1) * groups, tile, cols), jnp.bfloat16),
            pltpu.VMEM((groups, 3, tile, cols), jnp.bfloat16),
            pltpu.VMEM((tile, cols), jnp.bfloat16),
            pltpu.VMEM((tile, cols), jnp.bfloat16),
            pltpu.VMEM((tile, cols), jnp.bfloat16),
            pltpu.VMEM((8, cols), jnp.float32),
            pltpu.VMEM((shards, 8, 128), jnp.float32),
            pltpu.VMEM((plane, 8, 128), jnp.float32),
            dma((shards, groups)),
            dma((4,)),
            dma((2, max(DEPTH, groups))),
            dma((2, 2)),
            dma((2, max(count, share + (shards - 2) * (share // widest(tiles))))),
            dma((max(split(shards, tiles), 1) * groups,)),
            dma((max(split(shards, tiles), 1) * groups,)),
            dma((3,)),
            dma((groups,)),
            dma((groups,)),
            dma((2,)),
            dma((groups, tiles)),
            dma((1,)),
            dma((shards,)),
            dma((2,)),
            dma((1,)),
            dma((max(groups - 1, 1), tiles)),
        ],
        compiler_params=pltpu.CompilerParams(
            collective_id=0, has_side_effects=True, vmem_limit_bytes=34 * 2**20
        ),
    )(step, x, master, one, two, average)


def store_kernel(low, high, master, one, two, average, w, *rest):
    outs, sem = rest[:-1], rest[-1]
    half = low.shape[0]
    pairs = [(low, w.at[pl.ds(0, half)]), (high, w.at[pl.ds(half, half)])]
    pairs += zip((master, one, two, average), outs)
    copies = [pltpu.make_async_copy(src, dst, sem.at[n]) for n, (src, dst) in enumerate(pairs)]
    for copy in copies:
        copy.start()
    for copy in copies:
        copy.wait()


def store(low, high, *arrays):
    shape = (2 * low.shape[0],) + low.shape[1:]
    return pl.pallas_call(
        store_kernel,
        out_shape=[jax.ShapeDtypeStruct(shape, low.dtype)]
        + [jax.ShapeDtypeStruct(a.shape, a.dtype) for a in arrays],
        in_specs=[pl.BlockSpec(memory_space=pltpu.VMEM)] * (len(arrays) + 2),
        out_specs=[pl.BlockSpec(memory_space=pl.ANY)] * (len(arrays) + 1),
        scratch_shapes=[pltpu.SemaphoreType.DMA((len(arrays) + 2,))],
        compiler_params=pltpu.CompilerParams(vmem_limit_bytes=34 * 2**20),
    )(low, high, *arrays)


def body(sizes, limit, qkv_grad, master, moment_one, moment_two, average, step):
    shards, groups, _ = sizes
    rows = qkv_grad.shape[1] // (shards * groups)
    cols = qkv_grad.shape[2]
    parts = adam_step(
        sizes,
        limit,
        step.reshape(1),
        qkv_grad.reshape(shards, groups, rows, cols),
        master,
        moment_one,
        moment_two,
        average.reshape(groups, rows, cols),
    )
    weights, new_master, new_one, new_two, new_average = store(*parts)
    return (
        weights.reshape(shards * groups * rows, cols),
        new_master,
        new_one,
        new_two,
        new_average.reshape(average.shape),
    )


def solution(mesh):
    state = P(("section", "shard", "tensor"), None)
    in_specs = (
        P("shard", "section", "tensor"),
        state,
        state,
        state,
        P(("section", "shard"), "tensor"),
        P(),
    )
    out_specs = (
        P("section", "tensor"),
        state,
        state,
        state,
        P(("section", "shard"), "tensor"),
    )
    sizes = tuple(mesh.shape[name] for name in ("shard", "tensor", "section"))

    def run(qkv_grad, master, moment_one, moment_two, average, step):
        limit = math.sqrt(master.shape[0] * master.shape[1])
        fn = functools.partial(body, sizes, limit)
        return jax.shard_map(fn, mesh=mesh, in_specs=in_specs, out_specs=out_specs, check_vma=False)(
            qkv_grad, master, moment_one, moment_two, average, step
        )

    return run
```

```python
import functools
import math

import jax
import jax.numpy as jnp
from jax import lax
from jax.experimental import pallas as pl
from jax.experimental.pallas import tpu as pltpu
from jax.sharding import PartitionSpec as P

MESH = pl.DeviceIdType.MESH
DEPTH = 6
LAG = 2
KEPT = 1
WIDE = 4


def step_kernel(
    sizes, limit, step, x, master, one, two, average,
    w_low, w_high, out_master, out_one, out_two, out_average,
    held, inbox, gbox, half, extra, early, gtile, wtile, other, square, zbox, pbox,
    x_sem, state_sem, send, wide_send, recv, extra_send, extra_recv, early_load, early_send, early_recv, sum_send, sum_recv, z_send, z_recv, p_sem,
    y_send, y_recv,
):
    shards, groups, sections = sizes
    s, t, c = lax.axis_index("shard"), lax.axis_index("tensor"), lax.axis_index("section")
    last = shards - 1
    near = shards // 2
    _, _, rows, cols = x.shape
    tile = inbox.shape[2]
    tiles = rows // tile
    share = groups * tiles
    count = near * share
    plane = groups * sections
    depth = max(DEPTH, groups)
    wide = widest(tiles)
    blocks = share // wide
    at_end = jnp.logical_or(s == 0, s == last)
    at_near = jnp.logical_or(s == 1, s == last - 1)
    kept = split(shards, tiles)
    holders = [0, last] + ([1, last - 1] if kept else [])
    told = tiles - kept - 1
    seat = t * sections + c

    def load(q, g):
        return pltpu.make_async_copy(x.at[q, g], held.at[q, g], x_sem.at[q, g])

    def fetch(n):
        for g in range(groups):
            @pl.when(s > 0)
            def _():
                load(last - n, g).start()

            @pl.when(s < last)
            def _():
                load(n, g).start()

    states = [
        pltpu.make_async_copy(src, dst, state_sem.at[n])
        for n, (src, dst) in enumerate(
            ((master, out_master), (one, out_one), (two, out_two), (average, out_average))
        )
    ]

    barrier = pltpu.get_barrier_semaphore()

    def peer(off):
        at = lax.rem(seat + off, plane)
        return {"tensor": lax.div(at, sections), "section": lax.rem(at, sections)}

    @pl.loop(1, plane)
    def _(off):
        pl.semaphore_signal(barrier, inc=1, device_id=peer(off), device_id_type=MESH)

    @pl.loop(groups, shards * groups)
    def _(off):
        pl.semaphore_signal(
            barrier,
            inc=1,
            device_id={
                "shard": lax.rem(s + lax.div(off, groups), shards),
                "tensor": lax.rem(t + lax.rem(off, groups), groups),
            },
            device_id_type=MESH,
        )

    def part(j):
        return pl.ds(pl.multiple_of(j * tile, tile), tile)

    if kept:
        firsts = [
            pltpu.make_async_copy(src.at[part(told)], dst.at[part(told)], early_load.at[n])
            for n, (src, dst) in enumerate(((master, out_master), (one, out_one), (two, out_two)))
        ]

        @pl.when(at_near)
        def _():
            for copy in firsts:
                copy.start()

    fetch(0)
    square[...] = jnp.zeros_like(square)
    zbox[...] = jnp.zeros_like(zbox)

    def tell(k, first=0, size=3):
        return pltpu.make_async_remote_copy(
            src_ref=early.at[k, pl.ds(first, size)],
            dst_ref=early.at[t, pl.ds(first, size)],
            send_sem=early_send.at[k],
            recv_sem=early_recv.at[t],
            device_id={"shard": jnp.where(s == 1, 0, last), "tensor": lax.rem(t + k, groups)},
            device_id_type=MESH,
        )

    if kept:
        @pl.when(at_near)
        def _():
            for n, (copy, ref) in enumerate(zip(firsts, (out_master, out_one, out_two))):
                copy.wait()

                @pl.loop(0, groups)
                def _(k):
                    there = pl.ds(pl.multiple_of(lax.rem(t + k, groups) * cols, 128), cols)
                    early[k, n] = ref[part(told), there].astype(jnp.bfloat16)

    pl.semaphore_wait(barrier, plane - 1 + (shards - 1) * groups)

    if kept:
        @pl.when(at_near)
        def _():
            tell(0).start()


    def place(way, i):
        n, rest = lax.div(i, share), lax.rem(i, share)
        j, g = lax.div(rest, groups), lax.rem(rest, groups)
        return (last - n if way == 0 else n), g, j

    def short_of(way, q, j):
        return jnp.logical_and(q == (last - 1 if way == 0 else 1), j >= tiles - kept)

    def hop(way, i, src):
        return pltpu.make_async_remote_copy(
            src_ref=src,
            dst_ref=inbox.at[way, i],
            send_sem=send.at[way, lax.rem(i, depth)],
            recv_sem=recv.at[way, i],
            device_id={"shard": jnp.minimum(s + 1, last) if way == 0 else jnp.maximum(s - 1, 0)},
            device_id_type=MESH,
        )

    def spare(g, j, q=0):
        e = (j - (tiles - kept)) * groups + g
        return pltpu.make_async_remote_copy(
            src_ref=x.at[q, g, part(j)],
            dst_ref=extra.at[e],
            send_sem=extra_send.at[e],
            recv_sem=extra_recv.at[e],
            device_id={"shard": jnp.where(s == 0, 1, last - 1)},
            device_id_type=MESH,
        )

    def spares(use):
        for q, where in ((1, 0), (last - 1, last)):
            @pl.when(s == where)
            def _():
                for j in range(tiles - kept, tiles):
                    for g in range(groups):
                        use(spare(g, j, q))

    def hand(way, i):
        q, g, j = place(way, i)
        return pltpu.make_async_remote_copy(
            src_ref=inbox.at[way, i],
            dst_ref=gbox.at[t, part(j)],
            send_sem=sum_send.at[jnp.where(q == s, 0, 1)],
            recv_sem=sum_recv.at[t, j],
            device_id={"shard": q, "tensor": g},
            device_id_type=MESH,
        )

    def summed(g, j):
        return pltpu.make_async_remote_copy(
            src_ref=gbox.at[g, part(j)],
            dst_ref=gbox.at[g, part(j)],
            send_sem=sum_send.at[0],
            recv_sem=sum_recv.at[g, j],
            device_id={"tensor": g},
            device_id_type=MESH,
        )

    @pl.loop(0, count + LAG * last)
    def _(now):
        @pl.when(now == 1)
        def _():
            for n in range(1, near):
                fetch(n)

        @pl.when(now == LAG * last)
        def _():
            for copy in states:
                copy.start()

        for way in (0, 1):
            lag = s if way == 0 else last - s
            i = now - LAG * lag
            q, g, j = place(way, i)
            cut = short_of(way, q, j)
            stop = jnp.where(cut, last - 1, last)

            def finish(acc):
                short = acc.astype(jnp.bfloat16)
                square[...] += jnp.sum((acc * acc).reshape(tile // 8, 8, cols), axis=0)
                mine = jnp.logical_and(q == s, g == t)

                @pl.when(mine)
                def _():
                    gbox[t, part(j)] = short

                @pl.when(jnp.logical_not(mine))
                def _():
                    inbox[way, i] = short

                @pl.when(jnp.logical_and(q == s, g != t))
                def _():
                    hand(way, i).start()

            @pl.when(jnp.logical_and(jnp.logical_and(i >= 0, i < count), lag <= stop))
            def _():
                before_q, _, before_j = place(way, i - depth)
                before_cut = short_of(way, before_q, before_j)
                before_stop = jnp.where(before_cut, last - 1, last)

                @pl.when(jnp.logical_and(lag < before_stop, i >= depth))
                def _():
                    hop(way, i - depth, inbox.at[way, i - depth]).wait_send()

                @pl.when(lag == 0)
                def _():
                    hop(way, i, x.at[q, g, part(j)]).start()

                @pl.when(lag > 0)
                def _():
                    @pl.when(j == 0)
                    def _():
                        load(q, g).wait()

                    hop(way, i, inbox.at[way, i]).wait_recv()
                    acc = inbox[way, i].astype(jnp.float32) + held[q, g, part(j)].astype(jnp.float32)

                    @pl.when(lag < stop)
                    def _():
                        inbox[way, i] = acc.astype(jnp.bfloat16)
                        hop(way, i, inbox.at[way, i]).start()

                    @pl.when(jnp.logical_and(lag == stop, jnp.logical_not(cut)))
                    def _():
                        finish(acc)

                    if kept:
                        @pl.when(jnp.logical_and(lag == stop, cut))
                        def _():
                            spare(g, j).wait_recv()
                            e = (j - (tiles - kept)) * groups + g
                            finish(acc + extra[e].astype(jnp.float32))

        if kept:
            @pl.when(now == count - 1)
            def _():
                spares(lambda copy: copy.start())

            @pl.when(jnp.logical_and(now == count - kept * groups + LAG * (last - 1), at_near))
            def _():
                @pl.loop(1, groups)
                def _(k):
                    tell(k, 0, 1).start()

    def spread(off):
        return pltpu.make_async_remote_copy(
            src_ref=zbox.at[s],
            dst_ref=zbox.at[s],
            send_sem=z_send.at[0],
            recv_sem=z_recv.at[s],
            device_id={"shard": lax.rem(s + off, shards)},
            device_id_type=MESH,
        )

    def level(off):
        return pltpu.make_async_remote_copy(
            src_ref=pbox.at[seat],
            dst_ref=pbox.at[seat],
            send_sem=p_sem.at[0],
            recv_sem=p_sem.at[1],
            device_id=peer(off),
            device_id_type=MESH,
        )

    def settled(ref, sem):
        return pltpu.make_async_copy(ref, ref, sem)

    others = pbox.at[pl.ds(0, plane - 1)]

    def came(slot):
        return pltpu.make_async_copy(zbox.at[slot], zbox.at[slot], z_recv.at[slot])

    holding = jnp.logical_or(at_end, at_near) if kept else at_end

    @pl.when(holding)
    def _():
        narrow = square[:, :128]
        for n in range(1, cols // 128):
            narrow = narrow + square[:, n * 128 : (n + 1) * 128]
        zbox[s] = narrow

        @pl.loop(1, shards)
        def _(off):
            spread(off).start()

    for way, where in ((0, last), (1, 0)):
        @pl.when(s == where)
        def _():
            @pl.loop(share, count)
            def _(i):
                q, _, j = place(way, i)

                @pl.when(jnp.logical_not(short_of(way, q, j)))
                def _():
                    hand(way, i).start()

    for holder in holders:
        @pl.when(s != holder)
        def _():
            came(holder).wait()

    total = zbox[holders[0]]
    for holder in holders[1:]:
        total = total + zbox[holder]
    pbox[seat] = total

    for off in range(1, plane):
        level(off).start()

    if kept:
        @pl.when(at_near)
        def _():
            @pl.loop(1, groups)
            def _(k):
                tell(k, 1, 2).start()

    for way, here in ((0, s < last), (1, s > 0)):
        @pl.when(here)
        def _():
            @pl.loop(max(count - depth, 0), count)
            def _(i):
                q, _, j = place(way, i)
                lag = s if way == 0 else last - s

                @pl.when(lag < jnp.where(short_of(way, q, j), last - 1, last))
                def _():
                    hop(way, i, inbox.at[way, i]).wait_send()

    for copy in states:
        copy.wait()
    times = jnp.full((8, 128), step[0].astype(jnp.float32))
    first_fix = (1.0 / (1.0 - jnp.exp(times * math.log(0.9))))[:1, :1]
    second_fix = (1.0 / (1.0 - jnp.exp(times * math.log(0.95))))[:1, :1]

    settled(others, p_sem.at[1]).wait()

    whole = pbox[0]
    for n in range(1, plane):
        whole = whole + pbox[n]
    norm = jnp.sqrt(jnp.sum(jnp.sum(whole, axis=0, keepdims=True), axis=1, keepdims=True))
    clip = jnp.minimum(1.0, limit / (norm + 1e-06))

    def within(p, use):
        @pl.when(p < near)
        def _():
            use(w_low, p)

        @pl.when(p >= near)
        def _():
            use(w_high, p - near)

    def cross(k, j, w=w_low, row=0):
        return pltpu.make_async_remote_copy(
            src_ref=half.at[k - 1, part(j)],
            dst_ref=w.at[row, t, part(j)],
            send_sem=y_send.at[0],
            recv_sem=y_recv.at[k - 1, j],
            device_id={"tensor": lax.rem(t + k, groups)},
            device_id_type=MESH,
        )

    def crossed(k, j):
        g = lax.rem(t + k, groups)
        return pltpu.make_async_remote_copy(
            src_ref=w_low.at[0, g, part(j)],
            dst_ref=w_low.at[0, g, part(j)],
            send_sem=y_send.at[0],
            recv_sem=y_recv.at[groups - k - 1, j],
            device_id={"tensor": g},
            device_id_type=MESH,
        )

    def row_at(place):
        return lax.rem(place + tiles - kept, tiles)

    def onward(way):
        return jnp.minimum(s + 1, last) if way == 0 else jnp.maximum(s - 1, 0)

    def emit(way, n, w=w_low, row=0):
        j, k = row_at(lax.div(n, groups)), lax.rem(n, groups)
        block = w.at[row, lax.rem(t + k, groups), part(j)]
        return pltpu.make_async_remote_copy(
            src_ref=block,
            dst_ref=block,
            send_sem=send.at[way, lax.rem(n, depth)],
            recv_sem=recv.at[way, n],
            device_id={"shard": onward(way)},
            device_id_type=MESH,
        )

    def forward(way, n, w=w_low, row=0):
        b = lax.rem(n, blocks)
        j, k = lax.div(b, groups), lax.rem(b, groups)
        block = w.at[row, lax.rem(t + k, groups), pl.ds(pl.multiple_of(j * wide * tile, wide * tile), wide * tile)]
        return pltpu.make_async_remote_copy(
            src_ref=block,
            dst_ref=block,
            send_sem=wide_send.at[way, lax.rem(n, 2)],
            recv_sem=recv.at[way, share + n],
            device_id={"shard": onward(way)},
            device_id_type=MESH,
        )

    def sent(way, n):
        ends_next = s == (last - 1 if way == 0 else 1)
        return jnp.logical_not(
            jnp.logical_and(jnp.logical_and(ends_next, row_at(lax.div(n, groups)) == told), kept > 0)
        )

    def both(n):
        for way in (0, 1):
            @pl.when(s < last if way == 0 else s > 0)
            def _():
                @pl.when(jnp.logical_and(n >= depth, sent(way, n - depth)))
                def _():
                    emit(way, n - depth).wait_send()

                @pl.when(sent(way, n))
                def _():
                    within(s, lambda w, row: emit(way, n, w, row).start())

    def relay(way, n):
        reach = s if way == 0 else last - s

        @pl.when(n < reach * blocks)
        def _():
            @pl.when(n < blocks)
            def _():
                j, k = lax.div(n, groups), lax.rem(n, groups)
                for e in range(wide):
                    row = j * wide + e

                    @pl.when(jnp.logical_not(jnp.logical_and(jnp.logical_and(at_end, row == told), kept > 0)))
                    def _():
                        emit(way, lax.rem(row + kept, tiles) * groups + k).wait_recv()

            @pl.when(n >= blocks)
            def _():
                forward(way, n - blocks).wait_recv()

            @pl.when(s < last if way == 0 else s > 0)
            def _():
                @pl.when(n >= 2)
                def _():
                    forward(way, n - 2).wait_send()

                away = lax.div(n, blocks) + 1
                p = s - away if way == 0 else s + away
                within(p, lambda w, row: forward(way, n, w, row).start())

    def adam(grad, old, first, second):
        clipped = clip * grad.astype(jnp.float32)
        new_one = 0.9 * first + 0.1 * clipped
        new_two = 0.95 * second + 0.05 * clipped * clipped
        update = new_one * first_fix / (jnp.sqrt(new_two * second_fix) + 1e-08)
        return old * (1.0 - 0.1 * 0.1) - 0.1 * update, new_one, new_two

    @pl.loop(0, share + groups)
    def _(now):
        j, k = row_at(lax.div(now, groups)), lax.rem(now, groups)
        g = lax.rem(t + k, groups)

        @pl.when(now < share)
        def _():
            there = pl.ds(pl.multiple_of(g * cols, 128), cols)

            local = jnp.logical_or(at_end, jnp.logical_and(at_near, j >= tiles - kept)) if kept else at_end

            @pl.when(jnp.logical_not(jnp.logical_and(local, k == 0)))
            def _():
                summed(g, j).wait_recv()

            new_master, new_one, new_two = adam(
                gbox[g, part(j)], out_master[part(j), there], out_one[part(j), there], out_two[part(j), there]
            )
            out_one[part(j), there] = new_one
            out_two[part(j), there] = new_two
            out_master[part(j), there] = new_master
            wtile[...] = new_master.astype(jnp.bfloat16)

            if kept:
                @pl.when(jnp.logical_and(jnp.logical_or(at_end, at_near), j == told))
                def _():
                    @pl.when(at_near)
                    def _():
                        gtile[...] = gbox[g, part(j)]

                    @pl.when(at_end)
                    def _():
                        settled(early.at[k], early_recv.at[k]).wait()
                        gtile[...] = inbox[jnp.where(s == 0, 1, 0), share + told * groups + k]
                        other[...] = wtile[...]

                    rough = [early[k, n].astype(jnp.float32) for n in range(3)]
                    wtile[...] = adam(gtile[...], *rough)[0].astype(jnp.bfloat16)

                    @pl.when(at_end)
                    def _():
                        def keep(w, row):
                            w[row, k, part(j)] = wtile[...]

                        within(jnp.where(s == 0, 1, last - 1), keep)
                        wtile[...] = other[...]

            short = wtile[...]

            @pl.when(k == 0)
            def _():
                def keep(w, row):
                    w[row, t, part(j)] = short

                within(s, keep)
                both(now)

            @pl.when(k > 0)
            def _():
                half[k - 1, part(j)] = short
                within(s, lambda w, row: cross(k, j, w, row).start())

        @pl.when(jnp.logical_and(k > 0, now >= groups))
        def _():
            crossed(k, row_at(lax.div(now, groups) - 1)).wait_recv()
            both(now - groups)

    @pl.loop(0, last * blocks)
    def _(n):
        @pl.when(s < near)
        def _():
            relay(1, n)
            relay(0, n)

        @pl.when(s >= near)
        def _():
            relay(0, n)
            relay(1, n)

        @pl.when(n < blocks)
        def _():
            @pl.loop(0, wide)
            def _(e):
                m = n * wide + e
                j, g = lax.div(m, groups), lax.rem(m, groups)

                def mix(w, row):
                    fresh = w[row, g, part(j)].astype(jnp.float32)
                    out_average[g, part(j)] = 0.99 * out_average[g, part(j)] + 0.01 * fresh

                within(s, mix)

    for way in (0, 1):
        reach = s if way == 0 else last - s

        @pl.when(s < last if way == 0 else s > 0)
        def _():
            @pl.loop(max(share - depth, 0), share)
            def _(n):
                @pl.when(sent(way, n))
                def _():
                    emit(way, n).wait_send()

            for n in (2, 1):
                @pl.when(reach * blocks >= n)
                def _():
                    forward(way, reach * blocks - n).wait_send()

    if groups > 1:
        settled(half, y_send.at[0]).wait()

        @pl.when(at_end)
        def _():
            settled(inbox.at[0, pl.ds(0, tiles * (groups - 1))], sum_send.at[0]).wait()

    late = count - share - kept * groups
    if late:
        @pl.when(at_end)
        def _():
            settled(inbox.at[0, pl.ds(0, late)], sum_send.at[1]).wait()

    if kept:
        spares(lambda copy: copy.wait_send())

        @pl.when(at_near)
        def _():
            @pl.loop(0, groups)
            def _(k):
                tell(k).wait_send()

        if groups > 1:
            @pl.when(at_near)
            def _():
                settled(inbox.at[0, pl.ds(0, kept * (groups - 1))], sum_send.at[0]).wait()

    @pl.when(holding)
    def _():
        settled(zbox.at[pl.ds(0, last)], z_send.at[0]).wait()

    settled(others, p_sem.at[0]).wait()


def widest(tiles):
    return next(n for n in (WIDE, 2, 1) if tiles % n == 0)


def split(shards, tiles):
    return KEPT if shards >= 4 and tiles > KEPT else 0


def adam_step(sizes, limit, step, x, master, one, two, average):
    shards, groups, sections = sizes
    _, _, rows, cols = x.shape
    tile = min(rows, 16)
    tiles = rows // tile
    share = groups * tiles
    count = shards // 2 * share
    plane = groups * sections
    dma = pltpu.SemaphoreType.DMA
    anywhere = pl.BlockSpec(memory_space=pl.ANY)
    near = pl.BlockSpec(memory_space=pltpu.VMEM)
    state = jax.ShapeDtypeStruct(master.shape, jnp.float32)
    weights = jax.ShapeDtypeStruct((shards // 2,) + x.shape[1:], jnp.bfloat16)
    return pl.pallas_call(
        functools.partial(step_kernel, sizes, limit),
        out_shape=[
            weights,
            weights,
            state,
            state,
            state,
            jax.ShapeDtypeStruct(average.shape, jnp.float32),
        ],
        in_specs=[pl.BlockSpec(memory_space=pltpu.SMEM)] + [anywhere] * 5,
        out_specs=[near] * 6,
        scratch_shapes=[
            pltpu.VMEM(x.shape, jnp.bfloat16),
            pltpu.VMEM((2, count, tile, cols), jnp.bfloat16),
            pltpu.VMEM((groups, rows, cols), jnp.bfloat16),
            pltpu.VMEM((max(groups - 1, 1), rows, cols), jnp.bfloat16),
            pltpu.VMEM((max(split(shards, tiles), 1) * groups, tile, cols), jnp.bfloat16),
            pltpu.VMEM((groups, 3, tile, cols), jnp.bfloat16),
            pltpu.VMEM((tile, cols), jnp.bfloat16),
            pltpu.VMEM((tile, cols), jnp.bfloat16),
            pltpu.VMEM((tile, cols), jnp.bfloat16),
            pltpu.VMEM((8, cols), jnp.float32),
            pltpu.VMEM((shards, 8, 128), jnp.float32),
            pltpu.VMEM((plane, 8, 128), jnp.float32),
            dma((shards, groups)),
            dma((4,)),
            dma((2, max(DEPTH, groups))),
            dma((2, 2)),
            dma((2, max(count, share + (shards - 2) * (share // widest(tiles))))),
            dma((max(split(shards, tiles), 1) * groups,)),
            dma((max(split(shards, tiles), 1) * groups,)),
            dma((3,)),
            dma((groups,)),
            dma((groups,)),
            dma((2,)),
            dma((groups, tiles)),
            dma((1,)),
            dma((shards,)),
            dma((2,)),
            dma((1,)),
            dma((max(groups - 1, 1), tiles)),
        ],
        compiler_params=pltpu.CompilerParams(
            collective_id=0, has_side_effects=True, vmem_limit_bytes=34 * 2**20
        ),
    )(step, x, master, one, two, average)


def store_kernel(low, high, master, one, two, average, w, *rest):
    outs, sem = rest[:-1], rest[-1]
    half = low.shape[0]
    pairs = [(low, w.at[pl.ds(0, half)]), (high, w.at[pl.ds(half, half)])]
    pairs += zip((master, one, two, average), outs)
    copies = [pltpu.make_async_copy(src, dst, sem.at[n]) for n, (src, dst) in enumerate(pairs)]
    for copy in copies:
        copy.start()
    for copy in copies:
        copy.wait()


def store(low, high, *arrays):
    shape = (2 * low.shape[0],) + low.shape[1:]
    return pl.pallas_call(
        store_kernel,
        out_shape=[jax.ShapeDtypeStruct(shape, low.dtype)]
        + [jax.ShapeDtypeStruct(a.shape, a.dtype) for a in arrays],
        in_specs=[pl.BlockSpec(memory_space=pltpu.VMEM)] * (len(arrays) + 2),
        out_specs=[pl.BlockSpec(memory_space=pl.ANY)] * (len(arrays) + 1),
        scratch_shapes=[pltpu.SemaphoreType.DMA((len(arrays) + 2,))],
        compiler_params=pltpu.CompilerParams(vmem_limit_bytes=34 * 2**20),
    )(low, high, *arrays)


def body(sizes, limit, qkv_grad, master, moment_one, moment_two, average, step):
    shards, groups, _ = sizes
    rows = qkv_grad.shape[1] // (shards * groups)
    cols = qkv_grad.shape[2]
    parts = adam_step(
        sizes,
        limit,
        step.reshape(1),
        qkv_grad.reshape(shards, groups, rows, cols),
        master,
        moment_one,
        moment_two,
        average.reshape(groups, rows, cols),
    )
    weights, new_master, new_one, new_two, new_average = store(*parts)
    return (
        weights.reshape(shards * groups * rows, cols),
        new_master,
        new_one,
        new_two,
        new_average.reshape(average.shape),
    )


def solution(mesh):
    state = P(("section", "shard", "tensor"), None)
    in_specs = (
        P("shard", "section", "tensor"),
        state,
        state,
        state,
        P(("section", "shard"), "tensor"),
        P(),
    )
    out_specs = (
        P("section", "tensor"),
        state,
        state,
        state,
        P(("section", "shard"), "tensor"),
    )
    sizes = tuple(mesh.shape[name] for name in ("shard", "tensor", "section"))

    def run(qkv_grad, master, moment_one, moment_two, average, step):
        limit = math.sqrt(master.shape[0] * master.shape[1])
        fn = functools.partial(body, sizes, limit)
        return jax.shard_map(fn, mesh=mesh, in_specs=in_specs, out_specs=out_specs, check_vma=False)(
            qkv_grad, master, moment_one, moment_two, average, step
        )

    return run
```

```python
import functools
import math

import jax
import jax.numpy as jnp
from jax import lax
from jax.experimental import pallas as pl
from jax.experimental.pallas import tpu as pltpu
from jax.sharding import PartitionSpec as P

MESH = pl.DeviceIdType.MESH
DEPTH = 10
LAG = 2
KEPT = 1
WIDE = 4


def step_kernel(
    sizes, limit, step, x, master, one, two, average,
    w_low, w_high, out_master, out_one, out_two, out_average,
    held, inbox, gbox, half, extra, early, gtile, wtile, other, square, zbox, pbox,
    x_sem, state_sem, send, wide_send, recv, extra_send, extra_recv, early_load, early_send, early_recv, sum_send, sum_recv, z_send, z_recv, p_sem,
    y_send, y_recv,
):
    shards, groups, sections = sizes
    s, t, c = lax.axis_index("shard"), lax.axis_index("tensor"), lax.axis_index("section")
    last = shards - 1
    near = shards // 2
    _, _, rows, cols = x.shape
    tile = inbox.shape[2]
    tiles = rows // tile
    share = groups * tiles
    count = near * share
    plane = groups * sections
    depth = max(DEPTH, groups)
    wide = widest(tiles)
    blocks = share // wide
    at_end = jnp.logical_or(s == 0, s == last)
    at_near = jnp.logical_or(s == 1, s == last - 1)
    kept = split(shards, tiles)
    holders = [0, last] + ([1, last - 1] if kept else [])
    told = tiles - kept - 1
    seat = t * sections + c

    def load(q, g):
        return pltpu.make_async_copy(x.at[q, g], held.at[q, g], x_sem.at[q, g])

    def fetch(n):
        for g in range(groups):
            @pl.when(s > 0)
            def _():
                load(last - n, g).start()

            @pl.when(s < last)
            def _():
                load(n, g).start()

    states = [
        pltpu.make_async_copy(src, dst, state_sem.at[n])
        for n, (src, dst) in enumerate(
            ((master, out_master), (one, out_one), (two, out_two), (average, out_average))
        )
    ]

    barrier = pltpu.get_barrier_semaphore()

    def peer(off):
        at = lax.rem(seat + off, plane)
        return {"tensor": lax.div(at, sections), "section": lax.rem(at, sections)}

    @pl.loop(1, plane)
    def _(off):
        pl.semaphore_signal(barrier, inc=1, device_id=peer(off), device_id_type=MESH)

    @pl.loop(groups, shards * groups)
    def _(off):
        pl.semaphore_signal(
            barrier,
            inc=1,
            device_id={
                "shard": lax.rem(s + lax.div(off, groups), shards),
                "tensor": lax.rem(t + lax.rem(off, groups), groups),
            },
            device_id_type=MESH,
        )

    def part(j):
        return pl.ds(pl.multiple_of(j * tile, tile), tile)

    if kept:
        firsts = [
            pltpu.make_async_copy(src.at[part(told)], dst.at[part(told)], early_load.at[n])
            for n, (src, dst) in enumerate(((master, out_master), (one, out_one), (two, out_two)))
        ]

        @pl.when(at_near)
        def _():
            for copy in firsts:
                copy.start()

    fetch(0)
    square[...] = jnp.zeros_like(square)
    zbox[...] = jnp.zeros_like(zbox)

    def tell(k, first=0, size=3):
        return pltpu.make_async_remote_copy(
            src_ref=early.at[k, pl.ds(first, size)],
            dst_ref=early.at[t, pl.ds(first, size)],
            send_sem=early_send.at[k],
            recv_sem=early_recv.at[t],
            device_id={"shard": jnp.where(s == 1, 0, last), "tensor": lax.rem(t + k, groups)},
            device_id_type=MESH,
        )

    if kept:
        @pl.when(at_near)
        def _():
            for n, (copy, ref) in enumerate(zip(firsts, (out_master, out_one, out_two))):
                copy.wait()

                @pl.loop(0, groups)
                def _(k):
                    there = pl.ds(pl.multiple_of(lax.rem(t + k, groups) * cols, 128), cols)
                    early[k, n] = ref[part(told), there].astype(jnp.bfloat16)

    pl.semaphore_wait(barrier, plane - 1 + (shards - 1) * groups)

    if kept:
        @pl.when(at_near)
        def _():
            for n in range(3):
                tell(0, n, 1).start()


    def place(way, i):
        n, rest = lax.div(i, share), lax.rem(i, share)
        j, g = lax.div(rest, groups), lax.rem(rest, groups)
        return (last - n if way == 0 else n), g, j

    def short_of(way, q, j):
        return jnp.logical_and(q == (last - 1 if way == 0 else 1), j >= tiles - kept)

    def hop(way, i, src):
        return pltpu.make_async_remote_copy(
            src_ref=src,
            dst_ref=inbox.at[way, i],
            send_sem=send.at[way, lax.rem(i, depth)],
            recv_sem=recv.at[way, i],
            device_id={"shard": jnp.minimum(s + 1, last) if way == 0 else jnp.maximum(s - 1, 0)},
            device_id_type=MESH,
        )

    def spare(g, j, q=0):
        e = (j - (tiles - kept)) * groups + g
        return pltpu.make_async_remote_copy(
            src_ref=x.at[q, g, part(j)],
            dst_ref=extra.at[e],
            send_sem=extra_send.at[e],
            recv_sem=extra_recv.at[e],
            device_id={"shard": jnp.where(s == 0, 1, last - 1)},
            device_id_type=MESH,
        )

    def spares(use):
        for q, where in ((1, 0), (last - 1, last)):
            @pl.when(s == where)
            def _():
                for j in range(tiles - kept, tiles):
                    for g in range(groups):
                        use(spare(g, j, q))

    def hand(way, i):
        q, g, j = place(way, i)
        return pltpu.make_async_remote_copy(
            src_ref=inbox.at[way, i],
            dst_ref=gbox.at[t, part(j)],
            send_sem=sum_send.at[jnp.where(q == s, 0, 1)],
            recv_sem=sum_recv.at[t, j],
            device_id={"shard": q, "tensor": g},
            device_id_type=MESH,
        )

    def summed(g, j):
        return pltpu.make_async_remote_copy(
            src_ref=gbox.at[g, part(j)],
            dst_ref=gbox.at[g, part(j)],
            send_sem=sum_send.at[0],
            recv_sem=sum_recv.at[g, j],
            device_id={"tensor": g},
            device_id_type=MESH,
        )

    @pl.loop(0, count + LAG * last)
    def _(now):
        @pl.when(now == 1)
        def _():
            for n in range(1, near):
                fetch(n)

        @pl.when(now == LAG * last)
        def _():
            for copy in states:
                copy.start()

        for way in (0, 1):
            lag = s if way == 0 else last - s
            i = now - LAG * lag
            q, g, j = place(way, i)
            cut = short_of(way, q, j)
            stop = jnp.where(cut, last - 1, last)

            def finish(acc):
                short = acc.astype(jnp.bfloat16)
                mine = jnp.logical_and(q == s, g == t)

                @pl.when(mine)
                def _():
                    gbox[t, part(j)] = short

                @pl.when(jnp.logical_not(mine))
                def _():
                    inbox[way, i] = short

                @pl.when(jnp.logical_and(q == s, g != t))
                def _():
                    hand(way, i).start()

                square[...] += jnp.sum((acc * acc).reshape(tile // 8, 8, cols), axis=0)

            @pl.when(jnp.logical_and(jnp.logical_and(i >= 0, i < count), lag <= stop))
            def _():
                before_q, _, before_j = place(way, i - depth)
                before_cut = short_of(way, before_q, before_j)
                before_stop = jnp.where(before_cut, last - 1, last)

                @pl.when(jnp.logical_and(lag < before_stop, i >= depth))
                def _():
                    hop(way, i - depth, inbox.at[way, i - depth]).wait_send()

                @pl.when(lag == 0)
                def _():
                    hop(way, i, x.at[q, g, part(j)]).start()

                @pl.when(lag > 0)
                def _():
                    @pl.when(j == 0)
                    def _():
                        load(q, g).wait()

                    hop(way, i, inbox.at[way, i]).wait_recv()
                    acc = inbox[way, i].astype(jnp.float32) + held[q, g, part(j)].astype(jnp.float32)

                    @pl.when(lag < stop)
                    def _():
                        inbox[way, i] = acc.astype(jnp.bfloat16)
                        hop(way, i, inbox.at[way, i]).start()

                    @pl.when(jnp.logical_and(lag == stop, jnp.logical_not(cut)))
                    def _():
                        finish(acc)

                    if kept:
                        @pl.when(jnp.logical_and(lag == stop, cut))
                        def _():
                            spare(g, j).wait_recv()
                            e = (j - (tiles - kept)) * groups + g
                            finish(acc + extra[e].astype(jnp.float32))

        if kept:
            @pl.when(now == count - 1)
            def _():
                spares(lambda copy: copy.start())

            @pl.when(jnp.logical_and(now == count - kept * groups + LAG * (last - 1), at_near))
            def _():
                @pl.loop(1, groups)
                def _(k):
                    tell(k, 0, 1).start()

    def spread(off):
        return pltpu.make_async_remote_copy(
            src_ref=zbox.at[s],
            dst_ref=zbox.at[s],
            send_sem=z_send.at[0],
            recv_sem=z_recv.at[s],
            device_id={"shard": lax.rem(s + off, shards)},
            device_id_type=MESH,
        )

    def level(off):
        return pltpu.make_async_remote_copy(
            src_ref=pbox.at[seat],
            dst_ref=pbox.at[seat],
            send_sem=p_sem.at[0],
            recv_sem=p_sem.at[1],
            device_id=peer(off),
            device_id_type=MESH,
        )

    def settled(ref, sem):
        return pltpu.make_async_copy(ref, ref, sem)

    others = pbox.at[pl.ds(0, plane - 1)]

    def came(slot):
        return pltpu.make_async_copy(zbox.at[slot], zbox.at[slot], z_recv.at[slot])

    holding = jnp.logical_or(at_end, at_near) if kept else at_end

    @pl.when(holding)
    def _():
        narrow = square[:, :128]
        for n in range(1, cols // 128):
            narrow = narrow + square[:, n * 128 : (n + 1) * 128]
        zbox[s] = narrow

        @pl.loop(1, shards)
        def _(off):
            spread(off).start()

    for way, where in ((0, last), (1, 0)):
        @pl.when(s == where)
        def _():
            @pl.loop(share, count)
            def _(i):
                q, _, j = place(way, i)

                @pl.when(jnp.logical_not(short_of(way, q, j)))
                def _():
                    hand(way, i).start()

    for holder in holders:
        @pl.when(s != holder)
        def _():
            came(holder).wait()

    total = zbox[holders[0]]
    for holder in holders[1:]:
        total = total + zbox[holder]
    pbox[seat] = total

    for off in range(1, plane):
        level(off).start()

    if kept:
        @pl.when(at_near)
        def _():
            @pl.loop(1, groups)
            def _(k):
                tell(k, 1, 2).start()

    for way, here in ((0, s < last), (1, s > 0)):
        @pl.when(here)
        def _():
            @pl.loop(max(count - depth, 0), count)
            def _(i):
                q, _, j = place(way, i)
                lag = s if way == 0 else last - s

                @pl.when(lag < jnp.where(short_of(way, q, j), last - 1, last))
                def _():
                    hop(way, i, inbox.at[way, i]).wait_send()

    for copy in states:
        copy.wait()
    times = jnp.full((8, 128), step[0].astype(jnp.float32))
    first_fix = (1.0 / (1.0 - jnp.exp(times * math.log(0.9))))[:1, :1]
    second_fix = (1.0 / (1.0 - jnp.exp(times * math.log(0.95))))[:1, :1]

    settled(others, p_sem.at[1]).wait()

    whole = pbox[0]
    for n in range(1, plane):
        whole = whole + pbox[n]
    norm = jnp.sqrt(jnp.sum(jnp.sum(whole, axis=0, keepdims=True), axis=1, keepdims=True))
    clip = jnp.minimum(1.0, limit / (norm + 1e-06))

    def within(p, use):
        @pl.when(p < near)
        def _():
            use(w_low, p)

        @pl.when(p >= near)
        def _():
            use(w_high, p - near)

    def cross(k, j, w=w_low, row=0):
        return pltpu.make_async_remote_copy(
            src_ref=half.at[k - 1, part(j)],
            dst_ref=w.at[row, t, part(j)],
            send_sem=y_send.at[0],
            recv_sem=y_recv.at[k - 1, j],
            device_id={"tensor": lax.rem(t + k, groups)},
            device_id_type=MESH,
        )

    def crossed(k, j):
        g = lax.rem(t + k, groups)
        return pltpu.make_async_remote_copy(
            src_ref=w_low.at[0, g, part(j)],
            dst_ref=w_low.at[0, g, part(j)],
            send_sem=y_send.at[0],
            recv_sem=y_recv.at[groups - k - 1, j],
            device_id={"tensor": g},
            device_id_type=MESH,
        )

    def row_at(place):
        return lax.rem(place + tiles - kept, tiles)

    def onward(way):
        return jnp.minimum(s + 1, last) if way == 0 else jnp.maximum(s - 1, 0)

    def emit(way, n, w=w_low, row=0):
        j, k = row_at(lax.div(n, groups)), lax.rem(n, groups)
        block = w.at[row, lax.rem(t + k, groups), part(j)]
        return pltpu.make_async_remote_copy(
            src_ref=block,
            dst_ref=block,
            send_sem=send.at[way, lax.rem(n, depth)],
            recv_sem=recv.at[way, n],
            device_id={"shard": onward(way)},
            device_id_type=MESH,
        )

    def forward(way, n, w=w_low, row=0):
        b = lax.rem(n, blocks)
        j, k = lax.div(b, groups), lax.rem(b, groups)
        block = w.at[row, lax.rem(t + k, groups), pl.ds(pl.multiple_of(j * wide * tile, wide * tile), wide * tile)]
        return pltpu.make_async_remote_copy(
            src_ref=block,
            dst_ref=block,
            send_sem=wide_send.at[way, lax.rem(n, 2)],
            recv_sem=recv.at[way, share + n],
            device_id={"shard": onward(way)},
            device_id_type=MESH,
        )

    def sent(way, n):
        ends_next = s == (last - 1 if way == 0 else 1)
        return jnp.logical_not(
            jnp.logical_and(jnp.logical_and(ends_next, row_at(lax.div(n, groups)) == told), kept > 0)
        )

    def out(way, n):
        @pl.when(s < last if way == 0 else s > 0)
        def _():
            @pl.when(jnp.logical_and(n >= depth, sent(way, n - depth)))
            def _():
                emit(way, n - depth).wait_send()

            @pl.when(sent(way, n))
            def _():
                within(s, lambda w, row: emit(way, n, w, row).start())

    def both(n):
        @pl.when(s < near)
        def _():
            out(1, n)
            out(0, n)

        @pl.when(s >= near)
        def _():
            out(0, n)
            out(1, n)

    def relay(way, n):
        reach = s if way == 0 else last - s

        @pl.when(n < reach * blocks)
        def _():
            @pl.when(n < blocks)
            def _():
                j, k = lax.div(n, groups), lax.rem(n, groups)
                for e in range(wide):
                    row = j * wide + e

                    @pl.when(jnp.logical_not(jnp.logical_and(jnp.logical_and(at_end, row == told), kept > 0)))
                    def _():
                        emit(way, lax.rem(row + kept, tiles) * groups + k).wait_recv()

            @pl.when(n >= blocks)
            def _():
                forward(way, n - blocks).wait_recv()

            @pl.when(s < last if way == 0 else s > 0)
            def _():
                @pl.when(n >= 2)
                def _():
                    forward(way, n - 2).wait_send()

                away = lax.div(n, blocks) + 1
                p = s - away if way == 0 else s + away
                within(p, lambda w, row: forward(way, n, w, row).start())

    def adam(grad, old, first, second):
        clipped = clip * grad.astype(jnp.float32)
        new_one = 0.9 * first + 0.1 * clipped
        new_two = 0.95 * second + 0.05 * clipped * clipped
        update = new_one * first_fix / (jnp.sqrt(new_two * second_fix) + 1e-08)
        return old * (1.0 - 0.1 * 0.1) - 0.1 * update, new_one, new_two

    @pl.loop(0, share + groups)
    def _(now):
        j, k = row_at(lax.div(now, groups)), lax.rem(now, groups)
        g = lax.rem(t + k, groups)

        @pl.when(now < share)
        def _():
            there = pl.ds(pl.multiple_of(g * cols, 128), cols)

            local = jnp.logical_or(at_end, jnp.logical_and(at_near, j >= tiles - kept)) if kept else at_end

            @pl.when(jnp.logical_not(jnp.logical_and(local, k == 0)))
            def _():
                summed(g, j).wait_recv()

            new_master, new_one, new_two = adam(
                gbox[g, part(j)], out_master[part(j), there], out_one[part(j), there], out_two[part(j), there]
            )
            out_one[part(j), there] = new_one
            out_two[part(j), there] = new_two
            out_master[part(j), there] = new_master
            wtile[...] = new_master.astype(jnp.bfloat16)

            if kept:
                @pl.when(jnp.logical_and(jnp.logical_or(at_end, at_near), j == told))
                def _():
                    @pl.when(at_near)
                    def _():
                        gtile[...] = gbox[g, part(j)]

                    @pl.when(at_end)
                    def _():
                        settled(early.at[k], early_recv.at[k]).wait()
                        gtile[...] = inbox[jnp.where(s == 0, 1, 0), share + told * groups + k]
                        other[...] = wtile[...]

                    rough = [early[k, n].astype(jnp.float32) for n in range(3)]
                    wtile[...] = adam(gtile[...], *rough)[0].astype(jnp.bfloat16)

                    @pl.when(at_end)
                    def _():
                        def keep(w, row):
                            w[row, k, part(j)] = wtile[...]

                        within(jnp.where(s == 0, 1, last - 1), keep)
                        wtile[...] = other[...]

            short = wtile[...]

            @pl.when(k == 0)
            def _():
                def keep(w, row):
                    w[row, t, part(j)] = short

                within(s, keep)
                both(now)

            @pl.when(k > 0)
            def _():
                half[k - 1, part(j)] = short
                within(s, lambda w, row: cross(k, j, w, row).start())

        @pl.when(jnp.logical_and(k > 0, now >= groups))
        def _():
            crossed(k, row_at(lax.div(now, groups) - 1)).wait_recv()
            both(now - groups)

    @pl.loop(0, last * blocks)
    def _(n):
        @pl.when(s < near)
        def _():
            relay(1, n)
            relay(0, n)

        @pl.when(s >= near)
        def _():
            relay(0, n)
            relay(1, n)

        @pl.when(n < blocks)
        def _():
            @pl.loop(0, wide)
            def _(e):
                m = n * wide + e
                j, g = lax.div(m, groups), lax.rem(m, groups)

                def mix(w, row):
                    fresh = w[row, g, part(j)].astype(jnp.float32)
                    out_average[g, part(j)] = 0.99 * out_average[g, part(j)] + 0.01 * fresh

                within(s, mix)

    for way in (0, 1):
        reach = s if way == 0 else last - s

        @pl.when(s < last if way == 0 else s > 0)
        def _():
            @pl.loop(max(share - depth, 0), share)
            def _(n):
                @pl.when(sent(way, n))
                def _():
                    emit(way, n).wait_send()

            for n in (2, 1):
                @pl.when(reach * blocks >= n)
                def _():
                    forward(way, reach * blocks - n).wait_send()

    if groups > 1:
        settled(half, y_send.at[0]).wait()

        @pl.when(at_end)
        def _():
            settled(inbox.at[0, pl.ds(0, tiles * (groups - 1))], sum_send.at[0]).wait()

    late = count - share - kept * groups
    if late:
        @pl.when(at_end)
        def _():
            settled(inbox.at[0, pl.ds(0, late)], sum_send.at[1]).wait()

    if kept:
        spares(lambda copy: copy.wait_send())

        @pl.when(at_near)
        def _():
            @pl.loop(0, groups)
            def _(k):
                tell(k).wait_send()

        if groups > 1:
            @pl.when(at_near)
            def _():
                settled(inbox.at[0, pl.ds(0, kept * (groups - 1))], sum_send.at[0]).wait()

    @pl.when(holding)
    def _():
        settled(zbox.at[pl.ds(0, last)], z_send.at[0]).wait()

    settled(others, p_sem.at[0]).wait()


def widest(tiles):
    return next(n for n in (WIDE, 2, 1) if tiles % n == 0)


def split(shards, tiles):
    return KEPT if shards >= 4 and tiles > KEPT else 0


def adam_step(sizes, limit, step, x, master, one, two, average):
    shards, groups, sections = sizes
    _, _, rows, cols = x.shape
    tile = min(rows, 16)
    tiles = rows // tile
    share = groups * tiles
    count = shards // 2 * share
    plane = groups * sections
    dma = pltpu.SemaphoreType.DMA
    anywhere = pl.BlockSpec(memory_space=pl.ANY)
    near = pl.BlockSpec(memory_space=pltpu.VMEM)
    state = jax.ShapeDtypeStruct(master.shape, jnp.float32)
    weights = jax.ShapeDtypeStruct((shards // 2,) + x.shape[1:], jnp.bfloat16)
    return pl.pallas_call(
        functools.partial(step_kernel, sizes, limit),
        out_shape=[
            weights,
            weights,
            state,
            state,
            state,
            jax.ShapeDtypeStruct(average.shape, jnp.float32),
        ],
        in_specs=[pl.BlockSpec(memory_space=pltpu.SMEM)] + [anywhere] * 5,
        out_specs=[near] * 6,
        scratch_shapes=[
            pltpu.VMEM(x.shape, jnp.bfloat16),
            pltpu.VMEM((2, count, tile, cols), jnp.bfloat16),
            pltpu.VMEM((groups, rows, cols), jnp.bfloat16),
            pltpu.VMEM((max(groups - 1, 1), rows, cols), jnp.bfloat16),
            pltpu.VMEM((max(split(shards, tiles), 1) * groups, tile, cols), jnp.bfloat16),
            pltpu.VMEM((groups, 3, tile, cols), jnp.bfloat16),
            pltpu.VMEM((tile, cols), jnp.bfloat16),
            pltpu.VMEM((tile, cols), jnp.bfloat16),
            pltpu.VMEM((tile, cols), jnp.bfloat16),
            pltpu.VMEM((8, cols), jnp.float32),
            pltpu.VMEM((shards, 8, 128), jnp.float32),
            pltpu.VMEM((plane, 8, 128), jnp.float32),
            dma((shards, groups)),
            dma((4,)),
            dma((2, max(DEPTH, groups))),
            dma((2, 2)),
            dma((2, max(count, share + (shards - 2) * (share // widest(tiles))))),
            dma((max(split(shards, tiles), 1) * groups,)),
            dma((max(split(shards, tiles), 1) * groups,)),
            dma((3,)),
            dma((groups,)),
            dma((groups,)),
            dma((2,)),
            dma((groups, tiles)),
            dma((1,)),
            dma((shards,)),
            dma((2,)),
            dma((1,)),
            dma((max(groups - 1, 1), tiles)),
        ],
        compiler_params=pltpu.CompilerParams(
            collective_id=0, has_side_effects=True, vmem_limit_bytes=34 * 2**20
        ),
    )(step, x, master, one, two, average)


def store_kernel(low, high, master, one, two, average, w, *rest):
    outs, sem = rest[:-1], rest[-1]
    half = low.shape[0]
    pairs = [(low, w.at[pl.ds(0, half)]), (high, w.at[pl.ds(half, half)])]
    pairs += zip((master, one, two, average), outs)
    copies = [pltpu.make_async_copy(src, dst, sem.at[n]) for n, (src, dst) in enumerate(pairs)]
    for copy in copies:
        copy.start()
    for copy in copies:
        copy.wait()


def store(low, high, *arrays):
    shape = (2 * low.shape[0],) + low.shape[1:]
    return pl.pallas_call(
        store_kernel,
        out_shape=[jax.ShapeDtypeStruct(shape, low.dtype)]
        + [jax.ShapeDtypeStruct(a.shape, a.dtype) for a in arrays],
        in_specs=[pl.BlockSpec(memory_space=pltpu.VMEM)] * (len(arrays) + 2),
        out_specs=[pl.BlockSpec(memory_space=pl.ANY)] * (len(arrays) + 1),
        scratch_shapes=[pltpu.SemaphoreType.DMA((len(arrays) + 2,))],
        compiler_params=pltpu.CompilerParams(vmem_limit_bytes=34 * 2**20),
    )(low, high, *arrays)


def body(sizes, limit, qkv_grad, master, moment_one, moment_two, average, step):
    shards, groups, _ = sizes
    rows = qkv_grad.shape[1] // (shards * groups)
    cols = qkv_grad.shape[2]
    parts = adam_step(
        sizes,
        limit,
        step.reshape(1),
        qkv_grad.reshape(shards, groups, rows, cols),
        master,
        moment_one,
        moment_two,
        average.reshape(groups, rows, cols),
    )
    weights, new_master, new_one, new_two, new_average = store(*parts)
    return (
        weights.reshape(shards * groups * rows, cols),
        new_master,
        new_one,
        new_two,
        new_average.reshape(average.shape),
    )


def solution(mesh):
    state = P(("section", "shard", "tensor"), None)
    in_specs = (
        P("shard", "section", "tensor"),
        state,
        state,
        state,
        P(("section", "shard"), "tensor"),
        P(),
    )
    out_specs = (
        P("section", "tensor"),
        state,
        state,
        state,
        P(("section", "shard"), "tensor"),
    )
    sizes = tuple(mesh.shape[name] for name in ("shard", "tensor", "section"))

    def run(qkv_grad, master, moment_one, moment_two, average, step):
        limit = math.sqrt(master.shape[0] * master.shape[1])
        fn = functools.partial(body, sizes, limit)
        return jax.shard_map(fn, mesh=mesh, in_specs=in_specs, out_specs=out_specs, check_vma=False)(
            qkv_grad, master, moment_one, moment_two, average, step
        )

    return run
```

```python
import functools
import math

import jax
import jax.numpy as jnp
from jax import lax
from jax.experimental import pallas as pl
from jax.experimental.pallas import tpu as pltpu
from jax.sharding import PartitionSpec as P

MESH = pl.DeviceIdType.MESH
DEPTH = 6
LAG = 2
KEPT = 1
WIDE = 4


def step_kernel(
    sizes, limit, step, x, master, one, two, average,
    w_low, w_high, out_master, out_one, out_two, out_average,
    held, inbox, gbox, half, extra, early, gtile, wtile, other, square, zbox, pbox,
    x_sem, state_sem, send, wide_send, recv, extra_send, extra_recv, early_load, early_send, early_recv, sum_send, sum_recv, z_send, z_recv, p_sem,
    y_send, y_recv,
):
    shards, groups, sections = sizes
    s, t, c = lax.axis_index("shard"), lax.axis_index("tensor"), lax.axis_index("section")
    last = shards - 1
    near = shards // 2
    _, _, rows, cols = x.shape
    tile = inbox.shape[2]
    tiles = rows // tile
    share = groups * tiles
    count = near * share
    plane = groups * sections
    depth = max(DEPTH, groups)
    wide = widest(tiles)
    blocks = share // wide
    at_end = jnp.logical_or(s == 0, s == last)
    at_near = jnp.logical_or(s == 1, s == last - 1)
    kept = split(shards, tiles)
    holders = [0, last] + ([1, last - 1] if kept else [])
    told = tiles - kept - 1
    seat = t * sections + c

    def load(q, g):
        return pltpu.make_async_copy(x.at[q, g], held.at[q, g], x_sem.at[q, g])

    def fetch(n):
        for g in range(groups):
            @pl.when(s > 0)
            def _():
                load(last - n, g).start()

            @pl.when(s < last)
            def _():
                load(n, g).start()

    states = ((master, out_master), (one, out_one), (two, out_two), (average, out_average))

    barrier = pltpu.get_barrier_semaphore()

    def peer(off):
        at = lax.rem(seat + off, plane)
        return {"tensor": lax.div(at, sections), "section": lax.rem(at, sections)}

    @pl.loop(1, plane)
    def _(off):
        pl.semaphore_signal(barrier, inc=1, device_id=peer(off), device_id_type=MESH)

    @pl.loop(groups, shards * groups)
    def _(off):
        pl.semaphore_signal(
            barrier,
            inc=1,
            device_id={
                "shard": lax.rem(s + lax.div(off, groups), shards),
                "tensor": lax.rem(t + lax.rem(off, groups), groups),
            },
            device_id_type=MESH,
        )

    def part(j):
        return pl.ds(pl.multiple_of(j * tile, tile), tile)

    if kept:
        firsts = [
            pltpu.make_async_copy(src.at[part(told)], dst.at[part(told)], early_load.at[n])
            for n, (src, dst) in enumerate(((master, out_master), (one, out_one), (two, out_two)))
        ]

        @pl.when(at_near)
        def _():
            for copy in firsts:
                copy.start()

    fetch(0)
    square[...] = jnp.zeros_like(square)
    zbox[...] = jnp.zeros_like(zbox)

    def tell(k, first=0, size=3):
        return pltpu.make_async_remote_copy(
            src_ref=early.at[k, pl.ds(first, size)],
            dst_ref=early.at[t, pl.ds(first, size)],
            send_sem=early_send.at[k],
            recv_sem=early_recv.at[t],
            device_id={"shard": jnp.where(s == 1, 0, last), "tensor": lax.rem(t + k, groups)},
            device_id_type=MESH,
        )

    if kept:
        @pl.when(at_near)
        def _():
            for n, (copy, ref) in enumerate(zip(firsts, (out_master, out_one, out_two))):
                copy.wait()

                @pl.loop(0, groups)
                def _(k):
                    there = pl.ds(pl.multiple_of(lax.rem(t + k, groups) * cols, 128), cols)
                    early[k, n] = ref[part(told), there].astype(jnp.bfloat16)

    pl.semaphore_wait(barrier, plane - 1 + (shards - 1) * groups)

    if kept:
        @pl.when(at_near)
        def _():
            tell(0).start()


    def place(way, i):
        n, rest = lax.div(i, share), lax.rem(i, share)
        j, g = lax.div(rest, groups), lax.rem(rest, groups)
        return (last - n if way == 0 else n), g, j

    def short_of(way, q, j):
        return jnp.logical_and(q == (last - 1 if way == 0 else 1), j >= tiles - kept)

    def hop(way, i, src):
        return pltpu.make_async_remote_copy(
            src_ref=src,
            dst_ref=inbox.at[way, i],
            send_sem=send.at[way, lax.rem(i, depth)],
            recv_sem=recv.at[way, i],
            device_id={"shard": jnp.minimum(s + 1, last) if way == 0 else jnp.maximum(s - 1, 0)},
            device_id_type=MESH,
        )

    def spare(g, j, q=0):
        e = (j - (tiles - kept)) * groups + g
        return pltpu.make_async_remote_copy(
            src_ref=x.at[q, g, part(j)],
            dst_ref=extra.at[e],
            send_sem=extra_send.at[e],
            recv_sem=extra_recv.at[e],
            device_id={"shard": jnp.where(s == 0, 1, last - 1)},
            device_id_type=MESH,
        )

    def spares(use):
        for q, where in ((1, 0), (last - 1, last)):
            @pl.when(s == where)
            def _():
                for j in range(tiles - kept, tiles):
                    for g in range(groups):
                        use(spare(g, j, q))

    def hand(way, i):
        q, g, j = place(way, i)
        return pltpu.make_async_remote_copy(
            src_ref=inbox.at[way, i],
            dst_ref=gbox.at[t, part(j)],
            send_sem=sum_send.at[jnp.where(q == s, 0, 1)],
            recv_sem=sum_recv.at[t, j],
            device_id={"shard": q, "tensor": g},
            device_id_type=MESH,
        )

    def summed(g, j):
        return pltpu.make_async_remote_copy(
            src_ref=gbox.at[g, part(j)],
            dst_ref=gbox.at[g, part(j)],
            send_sem=sum_send.at[0],
            recv_sem=sum_recv.at[g, j],
            device_id={"tensor": g},
            device_id_type=MESH,
        )

    @pl.loop(0, count + LAG * last)
    def _(now):
        @pl.when(now == 1)
        def _():
            for n in range(1, near):
                fetch(n)

        step_row = now - LAG * last

        @pl.when(jnp.logical_and(step_row >= 0, step_row < tiles))
        def _():
            for n, (src, dst) in enumerate(states[:3]):
                pltpu.make_async_copy(src.at[part(step_row)], dst.at[part(step_row)], state_sem.at[n]).start()
            pltpu.make_async_copy(
                average.at[:, part(step_row)], out_average.at[:, part(step_row)], state_sem.at[3]
            ).start()

        for way in (0, 1):
            lag = s if way == 0 else last - s
            i = now - LAG * lag
            q, g, j = place(way, i)
            cut = short_of(way, q, j)
            stop = jnp.where(cut, last - 1, last)

            def finish(acc):
                short = acc.astype(jnp.bfloat16)
                square[...] += jnp.sum((acc * acc).reshape(tile // 8, 8, cols), axis=0)
                mine = jnp.logical_and(q == s, g == t)

                @pl.when(mine)
                def _():
                    gbox[t, part(j)] = short

                @pl.when(jnp.logical_not(mine))
                def _():
                    inbox[way, i] = short

                @pl.when(jnp.logical_and(q == s, g != t))
                def _():
                    hand(way, i).start()

            @pl.when(jnp.logical_and(jnp.logical_and(i >= 0, i < count), lag <= stop))
            def _():
                before_q, _, before_j = place(way, i - depth)
                before_cut = short_of(way, before_q, before_j)
                before_stop = jnp.where(before_cut, last - 1, last)

                @pl.when(jnp.logical_and(lag < before_stop, i >= depth))
                def _():
                    hop(way, i - depth, inbox.at[way, i - depth]).wait_send()

                @pl.when(lag == 0)
                def _():
                    hop(way, i, x.at[q, g, part(j)]).start()

                @pl.when(lag > 0)
                def _():
                    @pl.when(j == 0)
                    def _():
                        load(q, g).wait()

                    hop(way, i, inbox.at[way, i]).wait_recv()
                    acc = inbox[way, i].astype(jnp.float32) + held[q, g, part(j)].astype(jnp.float32)

                    @pl.when(lag < stop)
                    def _():
                        inbox[way, i] = acc.astype(jnp.bfloat16)
                        hop(way, i, inbox.at[way, i]).start()

                    @pl.when(jnp.logical_and(lag == stop, jnp.logical_not(cut)))
                    def _():
                        finish(acc)

                    if kept:
                        @pl.when(jnp.logical_and(lag == stop, cut))
                        def _():
                            spare(g, j).wait_recv()
                            e = (j - (tiles - kept)) * groups + g
                            finish(acc + extra[e].astype(jnp.float32))

        if kept:
            @pl.when(now == count - 1)
            def _():
                spares(lambda copy: copy.start())

            @pl.when(jnp.logical_and(now == count - kept * groups + LAG * (last - 1), at_near))
            def _():
                @pl.loop(1, groups)
                def _(k):
                    tell(k, 0, 1).start()

    def spread(off):
        return pltpu.make_async_remote_copy(
            src_ref=zbox.at[s],
            dst_ref=zbox.at[s],
            send_sem=z_send.at[0],
            recv_sem=z_recv.at[s],
            device_id={"shard": lax.rem(s + off, shards)},
            device_id_type=MESH,
        )

    def level(off):
        return pltpu.make_async_remote_copy(
            src_ref=pbox.at[seat],
            dst_ref=pbox.at[seat],
            send_sem=p_sem.at[0],
            recv_sem=p_sem.at[1],
            device_id=peer(off),
            device_id_type=MESH,
        )

    def settled(ref, sem):
        return pltpu.make_async_copy(ref, ref, sem)

    others = pbox.at[pl.ds(0, plane - 1)]

    def came(slot):
        return pltpu.make_async_copy(zbox.at[slot], zbox.at[slot], z_recv.at[slot])

    holding = jnp.logical_or(at_end, at_near) if kept else at_end

    @pl.when(holding)
    def _():
        narrow = square[:, :128]
        for n in range(1, cols // 128):
            narrow = narrow + square[:, n * 128 : (n + 1) * 128]
        zbox[s] = narrow

        @pl.loop(1, shards)
        def _(off):
            spread(off).start()

    for way, where in ((0, last), (1, 0)):
        @pl.when(s == where)
        def _():
            @pl.loop(share, count)
            def _(i):
                q, _, j = place(way, i)

                @pl.when(jnp.logical_not(short_of(way, q, j)))
                def _():
                    hand(way, i).start()

    for holder in holders:
        @pl.when(s != holder)
        def _():
            came(holder).wait()

    total = zbox[holders[0]]
    for holder in holders[1:]:
        total = total + zbox[holder]
    pbox[seat] = total

    for off in range(1, plane):
        level(off).start()

    if kept:
        @pl.when(at_near)
        def _():
            @pl.loop(1, groups)
            def _(k):
                tell(k, 1, 2).start()

    for way, here in ((0, s < last), (1, s > 0)):
        @pl.when(here)
        def _():
            @pl.loop(max(count - depth, 0), count)
            def _(i):
                q, _, j = place(way, i)
                lag = s if way == 0 else last - s

                @pl.when(lag < jnp.where(short_of(way, q, j), last - 1, last))
                def _():
                    hop(way, i, inbox.at[way, i]).wait_send()

    for n, (_, dst) in enumerate(states):
        settled(dst, state_sem.at[n]).wait()
    times = jnp.full((8, 128), step[0].astype(jnp.float32))
    first_fix = (1.0 / (1.0 - jnp.exp(times * math.log(0.9))))[:1, :1]
    second_fix = (1.0 / (1.0 - jnp.exp(times * math.log(0.95))))[:1, :1]

    settled(others, p_sem.at[1]).wait()

    whole = pbox[0]
    for n in range(1, plane):
        whole = whole + pbox[n]
    norm = jnp.sqrt(jnp.sum(jnp.sum(whole, axis=0, keepdims=True), axis=1, keepdims=True))
    clip = jnp.minimum(1.0, limit / (norm + 1e-06))

    def within(p, use):
        @pl.when(p < near)
        def _():
            use(w_low, p)

        @pl.when(p >= near)
        def _():
            use(w_high, p - near)

    def cross(k, j, w=w_low, row=0):
        return pltpu.make_async_remote_copy(
            src_ref=half.at[k - 1, part(j)],
            dst_ref=w.at[row, t, part(j)],
            send_sem=y_send.at[0],
            recv_sem=y_recv.at[k - 1, j],
            device_id={"tensor": lax.rem(t + k, groups)},
            device_id_type=MESH,
        )

    def crossed(k, j):
        g = lax.rem(t + k, groups)
        return pltpu.make_async_remote_copy(
            src_ref=w_low.at[0, g, part(j)],
            dst_ref=w_low.at[0, g, part(j)],
            send_sem=y_send.at[0],
            recv_sem=y_recv.at[groups - k - 1, j],
            device_id={"tensor": g},
            device_id_type=MESH,
        )

    def row_at(place):
        return lax.rem(place + tiles - kept, tiles)

    def onward(way):
        return jnp.minimum(s + 1, last) if way == 0 else jnp.maximum(s - 1, 0)

    def emit(way, n, w=w_low, row=0):
        j, k = row_at(lax.div(n, groups)), lax.rem(n, groups)
        block = w.at[row, lax.rem(t + k, groups), part(j)]
        return pltpu.make_async_remote_copy(
            src_ref=block,
            dst_ref=block,
            send_sem=send.at[way, lax.rem(n, depth)],
            recv_sem=recv.at[way, n],
            device_id={"shard": onward(way)},
            device_id_type=MESH,
        )

    def forward(way, n, w=w_low, row=0):
        b = lax.rem(n, blocks)
        j, k = lax.div(b, groups), lax.rem(b, groups)
        block = w.at[row, lax.rem(t + k, groups), pl.ds(pl.multiple_of(j * wide * tile, wide * tile), wide * tile)]
        return pltpu.make_async_remote_copy(
            src_ref=block,
            dst_ref=block,
            send_sem=wide_send.at[way, lax.rem(n, 2)],
            recv_sem=recv.at[way, share + n],
            device_id={"shard": onward(way)},
            device_id_type=MESH,
        )

    def sent(way, n):
        ends_next = s == (last - 1 if way == 0 else 1)
        return jnp.logical_not(
            jnp.logical_and(jnp.logical_and(ends_next, row_at(lax.div(n, groups)) == told), kept > 0)
        )

    def both(n):
        for way in (0, 1):
            @pl.when(s < last if way == 0 else s > 0)
            def _():
                @pl.when(jnp.logical_and(n >= depth, sent(way, n - depth)))
                def _():
                    emit(way, n - depth).wait_send()

                @pl.when(sent(way, n))
                def _():
                    within(s, lambda w, row: emit(way, n, w, row).start())

    def relay(way, n):
        reach = s if way == 0 else last - s

        @pl.when(n < reach * blocks)
        def _():
            @pl.when(n < blocks)
            def _():
                j, k = lax.div(n, groups), lax.rem(n, groups)
                for e in range(wide):
                    row = j * wide + e

                    @pl.when(jnp.logical_not(jnp.logical_and(jnp.logical_and(at_end, row == told), kept > 0)))
                    def _():
                        emit(way, lax.rem(row + kept, tiles) * groups + k).wait_recv()

            @pl.when(n >= blocks)
            def _():
                forward(way, n - blocks).wait_recv()

            @pl.when(s < last if way == 0 else s > 0)
            def _():
                @pl.when(n >= 2)
                def _():
                    forward(way, n - 2).wait_send()

                away = lax.div(n, blocks) + 1
                p = s - away if way == 0 else s + away
                within(p, lambda w, row: forward(way, n, w, row).start())

    def adam(grad, old, first, second):
        clipped = clip * grad.astype(jnp.float32)
        new_one = 0.9 * first + 0.1 * clipped
        new_two = 0.95 * second + 0.05 * clipped * clipped
        update = new_one * first_fix / (jnp.sqrt(new_two * second_fix) + 1e-08)
        return old * (1.0 - 0.1 * 0.1) - 0.1 * update, new_one, new_two

    @pl.loop(0, share + groups)
    def _(now):
        j, k = row_at(lax.div(now, groups)), lax.rem(now, groups)
        g = lax.rem(t + k, groups)

        @pl.when(now < share)
        def _():
            there = pl.ds(pl.multiple_of(g * cols, 128), cols)

            local = jnp.logical_or(at_end, jnp.logical_and(at_near, j >= tiles - kept)) if kept else at_end

            @pl.when(jnp.logical_not(jnp.logical_and(local, k == 0)))
            def _():
                summed(g, j).wait_recv()

            new_master, new_one, new_two = adam(
                gbox[g, part(j)], out_master[part(j), there], out_one[part(j), there], out_two[part(j), there]
            )
            out_one[part(j), there] = new_one
            out_two[part(j), there] = new_two
            out_master[part(j), there] = new_master
            wtile[...] = new_master.astype(jnp.bfloat16)

            if kept:
                @pl.when(jnp.logical_and(jnp.logical_or(at_end, at_near), j == told))
                def _():
                    @pl.when(at_near)
                    def _():
                        gtile[...] = gbox[g, part(j)]

                    @pl.when(at_end)
                    def _():
                        settled(early.at[k], early_recv.at[k]).wait()
                        gtile[...] = inbox[jnp.where(s == 0, 1, 0), share + told * groups + k]
                        other[...] = wtile[...]

                    rough = [early[k, n].astype(jnp.float32) for n in range(3)]
                    wtile[...] = adam(gtile[...], *rough)[0].astype(jnp.bfloat16)

                    @pl.when(at_end)
                    def _():
                        def keep(w, row):
                            w[row, k, part(j)] = wtile[...]

                        within(jnp.where(s == 0, 1, last - 1), keep)
                        wtile[...] = other[...]

            short = wtile[...]

            @pl.when(k == 0)
            def _():
                def keep(w, row):
                    w[row, t, part(j)] = short

                within(s, keep)
                both(now)

            @pl.when(k > 0)
            def _():
                half[k - 1, part(j)] = short
                within(s, lambda w, row: cross(k, j, w, row).start())

        @pl.when(jnp.logical_and(k > 0, now >= groups))
        def _():
            crossed(k, row_at(lax.div(now, groups) - 1)).wait_recv()
            both(now - groups)

    @pl.loop(0, last * blocks)
    def _(n):
        @pl.when(s < near)
        def _():
            relay(1, n)
            relay(0, n)

        @pl.when(s >= near)
        def _():
            relay(0, n)
            relay(1, n)

        @pl.when(n < blocks)
        def _():
            @pl.loop(0, wide)
            def _(e):
                m = n * wide + e
                j, g = lax.div(m, groups), lax.rem(m, groups)

                def mix(w, row):
                    fresh = w[row, g, part(j)].astype(jnp.float32)
                    out_average[g, part(j)] = 0.99 * out_average[g, part(j)] + 0.01 * fresh

                within(s, mix)

    for way in (0, 1):
        reach = s if way == 0 else last - s

        @pl.when(s < last if way == 0 else s > 0)
        def _():
            @pl.loop(max(share - depth, 0), share)
            def _(n):
                @pl.when(sent(way, n))
                def _():
                    emit(way, n).wait_send()

            for n in (2, 1):
                @pl.when(reach * blocks >= n)
                def _():
                    forward(way, reach * blocks - n).wait_send()

    if groups > 1:
        settled(half, y_send.at[0]).wait()

        @pl.when(at_end)
        def _():
            settled(inbox.at[0, pl.ds(0, tiles * (groups - 1))], sum_send.at[0]).wait()

    late = count - share - kept * groups
    if late:
        @pl.when(at_end)
        def _():
            settled(inbox.at[0, pl.ds(0, late)], sum_send.at[1]).wait()

    if kept:
        spares(lambda copy: copy.wait_send())

        @pl.when(at_near)
        def _():
            @pl.loop(0, groups)
            def _(k):
                tell(k).wait_send()

        if groups > 1:
            @pl.when(at_near)
            def _():
                settled(inbox.at[0, pl.ds(0, kept * (groups - 1))], sum_send.at[0]).wait()

    @pl.when(holding)
    def _():
        settled(zbox.at[pl.ds(0, last)], z_send.at[0]).wait()

    settled(others, p_sem.at[0]).wait()


def widest(tiles):
    return next(n for n in (WIDE, 2, 1) if tiles % n == 0)


def split(shards, tiles):
    return KEPT if shards >= 4 and tiles > KEPT else 0


def adam_step(sizes, limit, step, x, master, one, two, average):
    shards, groups, sections = sizes
    _, _, rows, cols = x.shape
    tile = min(rows, 16)
    tiles = rows // tile
    share = groups * tiles
    count = shards // 2 * share
    plane = groups * sections
    dma = pltpu.SemaphoreType.DMA
    anywhere = pl.BlockSpec(memory_space=pl.ANY)
    near = pl.BlockSpec(memory_space=pltpu.VMEM)
    state = jax.ShapeDtypeStruct(master.shape, jnp.float32)
    weights = jax.ShapeDtypeStruct((shards // 2,) + x.shape[1:], jnp.bfloat16)
    return pl.pallas_call(
        functools.partial(step_kernel, sizes, limit),
        out_shape=[
            weights,
            weights,
            state,
            state,
            state,
            jax.ShapeDtypeStruct(average.shape, jnp.float32),
        ],
        in_specs=[pl.BlockSpec(memory_space=pltpu.SMEM)] + [anywhere] * 5,
        out_specs=[near] * 6,
        scratch_shapes=[
            pltpu.VMEM(x.shape, jnp.bfloat16),
            pltpu.VMEM((2, count, tile, cols), jnp.bfloat16),
            pltpu.VMEM((groups, rows, cols), jnp.bfloat16),
            pltpu.VMEM((max(groups - 1, 1), rows, cols), jnp.bfloat16),
            pltpu.VMEM((max(split(shards, tiles), 1) * groups, tile, cols), jnp.bfloat16),
            pltpu.VMEM((groups, 3, tile, cols), jnp.bfloat16),
            pltpu.VMEM((tile, cols), jnp.bfloat16),
            pltpu.VMEM((tile, cols), jnp.bfloat16),
            pltpu.VMEM((tile, cols), jnp.bfloat16),
            pltpu.VMEM((8, cols), jnp.float32),
            pltpu.VMEM((shards, 8, 128), jnp.float32),
            pltpu.VMEM((plane, 8, 128), jnp.float32),
            dma((shards, groups)),
            dma((4,)),
            dma((2, max(DEPTH, groups))),
            dma((2, 2)),
            dma((2, max(count, share + (shards - 2) * (share // widest(tiles))))),
            dma((max(split(shards, tiles), 1) * groups,)),
            dma((max(split(shards, tiles), 1) * groups,)),
            dma((3,)),
            dma((groups,)),
            dma((groups,)),
            dma((2,)),
            dma((groups, tiles)),
            dma((1,)),
            dma((shards,)),
            dma((2,)),
            dma((1,)),
            dma((max(groups - 1, 1), tiles)),
        ],
        compiler_params=pltpu.CompilerParams(
            collective_id=0, has_side_effects=True, vmem_limit_bytes=34 * 2**20
        ),
    )(step, x, master, one, two, average)


def store_kernel(low, high, master, one, two, average, w, *rest):
    outs, sem = rest[:-1], rest[-1]
    half = low.shape[0]
    pairs = [(low, w.at[pl.ds(0, half)]), (high, w.at[pl.ds(half, half)])]
    pairs += zip((master, one, two, average), outs)
    copies = [pltpu.make_async_copy(src, dst, sem.at[n]) for n, (src, dst) in enumerate(pairs)]
    for copy in copies:
        copy.start()
    for copy in copies:
        copy.wait()


def store(low, high, *arrays):
    shape = (2 * low.shape[0],) + low.shape[1:]
    return pl.pallas_call(
        store_kernel,
        out_shape=[jax.ShapeDtypeStruct(shape, low.dtype)]
        + [jax.ShapeDtypeStruct(a.shape, a.dtype) for a in arrays],
        in_specs=[pl.BlockSpec(memory_space=pltpu.VMEM)] * (len(arrays) + 2),
        out_specs=[pl.BlockSpec(memory_space=pl.ANY)] * (len(arrays) + 1),
        scratch_shapes=[pltpu.SemaphoreType.DMA((len(arrays) + 2,))],
        compiler_params=pltpu.CompilerParams(vmem_limit_bytes=34 * 2**20),
    )(low, high, *arrays)


def body(sizes, limit, qkv_grad, master, moment_one, moment_two, average, step):
    shards, groups, _ = sizes
    rows = qkv_grad.shape[1] // (shards * groups)
    cols = qkv_grad.shape[2]
    parts = adam_step(
        sizes,
        limit,
        step.reshape(1),
        qkv_grad.reshape(shards, groups, rows, cols),
        master,
        moment_one,
        moment_two,
        average.reshape(groups, rows, cols),
    )
    weights, new_master, new_one, new_two, new_average = store(*parts)
    return (
        weights.reshape(shards * groups * rows, cols),
        new_master,
        new_one,
        new_two,
        new_average.reshape(average.shape),
    )


def solution(mesh):
    state = P(("section", "shard", "tensor"), None)
    in_specs = (
        P("shard", "section", "tensor"),
        state,
        state,
        state,
        P(("section", "shard"), "tensor"),
        P(),
    )
    out_specs = (
        P("section", "tensor"),
        state,
        state,
        state,
        P(("section", "shard"), "tensor"),
    )
    sizes = tuple(mesh.shape[name] for name in ("shard", "tensor", "section"))

    def run(qkv_grad, master, moment_one, moment_two, average, step):
        limit = math.sqrt(master.shape[0] * master.shape[1])
        fn = functools.partial(body, sizes, limit)
        return jax.shard_map(fn, mesh=mesh, in_specs=in_specs, out_specs=out_specs, check_vma=False)(
            qkv_grad, master, moment_one, moment_two, average, step
        )

    return run
```
